128 devices in a mesh: dp: 8 (over x, core), seq: 16 (over z, y).
Axes of the slice: x: 4, y: 4, z: 4, core: 2. Of those that a mesh axis runs over, the one named last changes fastest.
Arguments:
- qkv: bfloat16 [3, 8, 2048, 16, 128], P(None, 'dp', 'seq'), may hold values from -6 to 6
- tile_mask: int32 [8, 16, 16], replicated, may hold values from 0 to 1, as said below
- d_out: bfloat16 [8, 2048, 3072], P('dp', 'seq'), may hold values from -6 to 6
- w_out: bfloat16 [16, 128, 3072], P('seq'), may hold values from -0.109375 to 0.109375
- momentum: float32 [16, 128, 3072], P('seq'), may hold values from -170 to 170
Outputs:
- grad_qkv: bfloat16 [3, 8, 2048, 16, 128], P(None, 'dp', 'seq')
- synced_momentum: bfloat16 [16, 128, 3072], P('seq')
- worker_error: float32 [8, 16, 128, 3072], P('dp', 'seq')
- server_error: float32 [16, 128, 3072], P('seq', 'dp')
The draws below stay inside these ranges and needn't reach their ends.
Inputs may be any that keep to these rules, and one draw needn't show every extreme that they name: tile_mask[g, i, j] is 1 exactly when tiles i and j, numbered frame by frame over 4 frames of 2 by 2 tiles, differ by at most a per-group reach in frames (0 to 2), in tile rows (0 or 1) and in tile columns (0 or 1); every tile sees itself.
All inputs are finite; a program needn't handle non-finite values. Where the reference program divides by a largest or mean magnitude, that divisor is 1e-20 or more.
Results may differ from the reference program's by a relative error of at most 0.0085.
Values may be sent and summed in bfloat16 or wider, within the bound.
A program may use at most 128 MiB of HBM per device.

```python
import math
import jax
import jax.numpy as jnp
from jax import lax

D = 3072
HEADS = 16
HEAD_DIM = 128
GROUPS = 8
TILE = 128
LENGTH = 2048
TILES = 16
SEQS = 8


def draw_qkv(key, part):
    values = jnp.clip(jax.random.normal(key, (3, SEQS, LENGTH, HEADS, HEAD_DIM), jnp.float32), -4.0, 4.0)
    return values.astype(jnp.bfloat16)


def draw_tile_mask(key, part):
    frame_reach = jax.random.randint(jax.random.fold_in(key, 21), (GROUPS,), 0, 3)
    row_reach = jax.random.randint(jax.random.fold_in(key, 22), (GROUPS,), 0, 2)
    column_reach = jax.random.randint(jax.random.fold_in(key, 23), (GROUPS,), 0, 2)
    tile_ids = jnp.arange(TILES)
    frame = tile_ids // 4
    tile_row = tile_ids % 4 // 2
    tile_column = tile_ids % 2
    near_frame = jnp.abs(frame[:, None] - frame[None, :])[None] <= frame_reach[:, None, None]
    near_row = jnp.abs(tile_row[:, None] - tile_row[None, :])[None] <= row_reach[:, None, None]
    near_column = jnp.abs(tile_column[:, None] - tile_column[None, :])[None] <= column_reach[:, None, None]
    return (near_frame & near_row & near_column).astype(jnp.int32)


def draw_momentum(key, part):
    noise = jnp.clip(jax.random.normal(key, (HEADS, HEAD_DIM, D), jnp.float32), -4.0, 4.0)
    row_scale = jnp.exp(jax.random.uniform(jax.random.fold_in(key, 31), (HEADS, HEAD_DIM, 1), jnp.float32, 0.0, math.log(10.0)))
    column_scale = jnp.exp(jax.random.uniform(jax.random.fold_in(key, 32), (1, 1, D), jnp.float32, 0.0, math.log(3.0)))
    return noise * row_scale * column_scale


def level_of(stream_key, extent, pieces, least, top_value):
    def one(position, shards_of):
        steps = jax.random.uniform(jax.random.fold_in(jax.random.fold_in(stream_key, 6), position), (shards_of,), jnp.float32, least / len(pieces), top_value / len(pieces))
        return jnp.repeat(jnp.exp(steps), extent[position] // shards_of).reshape((-1,) + (1,) * (len(extent) - position - 1))

    factor_of = one(*pieces[0])
    for cut in pieces[1:]:
        factor_of = factor_of * one(*cut)
    return factor_of


def gaussian(rng, dims, scale, limit, cuts=(), kind=jnp.bfloat16):
    values = scale * jax.random.normal(rng, dims, jnp.float32)
    if cuts:
        values = values * level_of(rng, dims, cuts, -0.22, 0.18)
    return jnp.clip(values, -limit, limit).astype(kind)


def setup_inputs(seed: int = 0) -> dict:
    splits = jax.random.split(jax.random.key(seed), 6)
    qkv = draw_qkv(jax.random.fold_in(splits[5], 71), 0)
    tile_mask = draw_tile_mask(jax.random.fold_in(splits[5], 71), 0)
    d_out = gaussian(splits[2], (SEQS, LENGTH, D), 1.0, 6.0, ((0, 8), (1, 16)))
    w_out = gaussian(splits[3], (HEADS, HEAD_DIM, D), D ** -0.5, 0.109375, ((0, 16),))
    momentum = draw_momentum(jax.random.fold_in(splits[5], 71), 0)
    return dict(qkv=qkv, tile_mask=tile_mask, d_out=d_out, w_out=w_out, momentum=momentum)


def one_head(inputs):
    query_head, key_head, value_head, cot_head, head_tiles = inputs
    inv_root = 1.0 / math.sqrt(HEAD_DIM)
    scores = jnp.dot(query_head, key_head.T, preferred_element_type=jnp.float32) * inv_root
    visible = jnp.repeat(jnp.repeat(head_tiles, TILE, axis=0), TILE, axis=1) > 0
    scores = jnp.where(visible, scores, -jnp.inf)
    row_top = lax.optimization_barrier(jnp.max(scores, axis=-1, keepdims=True))
    expo = jnp.exp(scores - row_top)
    probs = expo / lax.optimization_barrier(jnp.sum(expo, axis=-1, keepdims=True))
    probs_b = probs.astype(jnp.bfloat16)
    attended = jnp.dot(probs_b, value_head, preferred_element_type=jnp.float32).astype(jnp.bfloat16)
    delta = lax.optimization_barrier(jnp.sum(cot_head.astype(jnp.float32) * attended.astype(jnp.float32), axis=-1))
    grad_v = jnp.dot(probs_b.T, cot_head, preferred_element_type=jnp.float32).astype(jnp.bfloat16)
    dprobs = jnp.dot(cot_head, value_head.T, preferred_element_type=jnp.float32)
    dscores = (probs * (dprobs - delta[:, None])).astype(jnp.bfloat16)
    grad_q = (jnp.dot(dscores, key_head, preferred_element_type=jnp.float32) * inv_root).astype(jnp.bfloat16)
    grad_k = (jnp.dot(dscores.T, query_head, preferred_element_type=jnp.float32) * inv_root).astype(jnp.bfloat16)
    return (attended, grad_q, grad_k, grad_v)

def reference(qkv, tile_mask, d_out, w_out, momentum):
    group_of_head = jnp.arange(HEADS) // (HEADS // GROUPS)
    head_masks = tile_mask[group_of_head]

    def one_sequence(inputs):
        triple, cot_rows = inputs
        head_cot = jnp.einsum('ld,hed->lhe', cot_rows.astype(jnp.float32), w_out.astype(jnp.float32)).astype(jnp.bfloat16)
        attended, grad_q, grad_k, grad_v = lax.map(one_head, (jnp.transpose(triple[0], (1, 0, 2)), jnp.transpose(triple[1], (1, 0, 2)), jnp.transpose(triple[2], (1, 0, 2)), jnp.transpose(head_cot, (1, 0, 2)), head_masks))
        grad_weight = jnp.einsum('hle,ld->hed', attended.astype(jnp.float32), cot_rows.astype(jnp.float32))
        grads = jnp.transpose(jnp.stack([grad_q, grad_k, grad_v]), (0, 2, 1, 3))
        return (grads, grad_weight)
    grads, grad_weight = lax.map(one_sequence, (jnp.transpose(qkv, (1, 0, 2, 3, 4)), d_out))
    grad_qkv = jnp.transpose(grads, (1, 0, 2, 3, 4))
    worker_mom = 0.9 * momentum[None] + 0.1 * grad_weight
    worker_scale = lax.optimization_barrier(jnp.mean(jnp.abs(worker_mom), axis=(2, 3), keepdims=True)) + 1e-06
    sent = (worker_scale * jnp.tanh(worker_mom / worker_scale)).astype(jnp.bfloat16)
    worker_error = worker_mom - sent.astype(jnp.float32)
    averaged = lax.optimization_barrier(jnp.sum(sent.astype(jnp.float32), axis=0)) / SEQS
    blocks = averaged.reshape(HEADS, SEQS, HEAD_DIM // SEQS, D)
    server_scale = lax.optimization_barrier(jnp.mean(jnp.abs(blocks), axis=(2, 3), keepdims=True)) + 1e-06
    synced = (server_scale * jnp.tanh(blocks / server_scale)).astype(jnp.bfloat16)
    server_error = (blocks - synced.astype(jnp.float32)).reshape(HEADS, HEAD_DIM, D)
    return (grad_qkv, synced.reshape(HEADS, HEAD_DIM, D), worker_error, server_error)
```

```python
import functools
import math

import jax
import jax.numpy as jnp
from jax import lax
from jax.experimental import pallas as pl
from jax.experimental.pallas import tpu as pltpu
from jax.sharding import PartitionSpec as P

HEADS = 16
GROUPS = 8
TILE = 128
SIDE = 4
BLOCKS = SIDE * SIDE
HALF = TILE // 2
MESH = pl.DeviceIdType.MESH

ORDER = (
    (0, 0),
    (-1, 0), (1, 0), (0, -1), (0, 1),
    (-1, -1), (-1, 1), (1, -1), (1, 1),
    (2, 0), (0, 2),
    (2, -1), (2, 1), (-1, 2), (1, 2),
    (2, 2),
)
COLUMNS = (0, -1, 1, 2)


def wrap(position, offset):
    return lax.rem(position + (offset + SIDE), SIDE)


def pick(step, table):
    value = jnp.int32(table[0])
    for index, entry in enumerate(table):
        if index and entry != table[0]:
            value = jnp.where(step == index, jnp.int32(entry), value)
    return value


def nt(a, b):
    return lax.dot_general(a, b, (((1,), (1,)), ((), ())), preferred_element_type=jnp.float32)


def nn(a, b):
    return lax.dot_general(a, b, (((1,), (0,)), ((), ())), preferred_element_type=jnp.float32)


def tn(a, b):
    return lax.dot_general(a, b, (((0,), (0,)), ((), ())), preferred_element_type=jnp.float32)


class Gather:
    def __init__(self, buf, z, y, z_first, row0, sem0, send, recv):
        self.buf, self.z, self.y, self.z_first = buf, z, y, z_first
        self.row0, self.sem0, self.send, self.recv = row0, sem0, send, recv

    def block(self, a, b):
        dz, dy = (a, b) if self.z_first else (b, a)
        return wrap(self.z, dz) * SIDE + wrap(self.y, dy)

    def peer(self, a, b):
        return {"seq": self.block(a, b)}

    def copy(self, slot, block, lo, n, a, b):
        rows = self.buf.at[block, pl.ds(self.row0 + lo, n)]
        return pltpu.make_async_remote_copy(
            src_ref=rows,
            dst_ref=rows,
            send_sem=self.send.at[self.sem0 + slot],
            recv_sem=self.recv.at[self.sem0 + slot],
            device_id=self.peer(a, b),
            device_id_type=MESH,
        )

    def first(self, kind):
        if kind == 0:
            return self.copy(0, self.block(0, 0), 0, HALF, 1, 0)
        if kind == 1:
            return self.copy(1, self.block(0, 0), 0, HALF, -1, 0)
        if kind == 2:
            return self.copy(2, self.block(-1, 0), 0, HALF // 2, 1, 0)
        return self.copy(3, self.block(1, 0), HALF // 2, HALF // 2, -1, 0)

    def second(self, column, kind):
        slot = 4 + 4 * COLUMNS.index(column) + kind
        if kind == 0:
            return self.copy(slot, self.block(column, 0), 0, HALF, 0, 1)
        if kind == 1:
            return self.copy(slot, self.block(column, 0), 0, HALF, 0, -1)
        if kind == 2:
            return self.copy(slot, self.block(column, -1), 0, HALF // 2, 0, 1)
        return self.copy(slot, self.block(column, 1), HALF // 2, HALF // 2, 0, -1)


def kernel(
    inv_root,
    qkv_ref, dout_ref, w_ref, mask_ref,
    grads_ref, gw_ref,
    qkvbuf, dbuf, bias, dkt, dvt,
    q_send, q_recv, d_send, d_recv, local_sem,
):
    me = lax.axis_index("seq")
    z = me // SIDE
    y = lax.rem(me, SIDE)
    peers = [
        wrap(z, dz) * SIDE + wrap(y, dy)
        for dz in range(SIDE) for dy in range(SIDE) if (dz, dy) != (0, 0)
    ]
    sources = [
        wrap(z, -dz) * SIDE + wrap(y, -dy)
        for dz in range(SIDE) for dy in range(SIDE) if (dz, dy) != (0, 0)
    ]

    own_d = pltpu.make_async_copy(dout_ref, dbuf.at[me], local_sem.at[0])
    own_d.start()
    own_q = pltpu.make_async_copy(
        qkv_ref.at[:, me], qkvbuf.at[:, pl.ds(me * TILE, TILE)], local_sem.at[1]
    )
    own_q.start()

    barrier = pltpu.get_barrier_semaphore()
    for peer in peers:
        pl.semaphore_signal(barrier, inc=1, device_id={"seq": peer}, device_id_type=MESH)
    pl.semaphore_wait(barrier, len(peers))

    q_copies = []
    for index, peer in enumerate(peers):
        copy = pltpu.make_async_remote_copy(
            src_ref=qkv_ref.at[:, peer],
            dst_ref=qkvbuf.at[:, pl.ds(me * TILE, TILE)],
            send_sem=q_send.at[index],
            recv_sem=q_recv.at[index],
            device_id={"seq": peer},
            device_id_type=MESH,
        )
        copy.start()
        q_copies.append(copy)

    halves = (
        Gather(dbuf, z, y, True, 0, 0, d_send, d_recv),
        Gather(dbuf, z, y, False, HALF, 20, d_send, d_recv),
    )
    own_d.wait()
    for g in halves:
        g.first(0).start()
        g.first(1).start()
    for g in halves:
        g.second(0, 0).start()
        g.second(0, 1).start()

    group = me // (HEADS // GROUPS)
    tiles = mask_ref[group]
    for j in range(BLOCKS):
        bias[:, j * TILE:(j + 1) * TILE] = jnp.broadcast_to(
            jnp.where(tiles[:, j:j + 1] > 0, 0.0, -jnp.inf), (BLOCKS, TILE)
        )
    dkt[...] = jnp.zeros_like(dkt)
    dvt[...] = jnp.zeros_like(dvt)
    gw_ref[...] = jnp.zeros_like(gw_ref)

    own_q.wait()
    for index, copy in enumerate(q_copies):
        copy.wait_recv()

    def arrive(step):
        if step == 1:
            for g in halves:
                g.first(0).wait_recv()
                g.first(2).start()
                g.second(-1, 0).start()
                g.second(-1, 1).start()
            for g in halves:
                g.first(1).wait_recv()
                g.first(3).start()
                g.second(1, 0).start()
                g.second(1, 1).start()
            for g in halves:
                g.second(0, 0).wait_recv()
                g.second(0, 2).start()
                g.second(0, 1).wait_recv()
                g.second(0, 3).start()
        elif step == 2:
            for g in halves:
                g.first(2).wait_recv()
                g.first(3).wait_recv()
                g.second(2, 0).start()
                g.second(2, 1).start()
        elif step == 5:
            for column in (-1, 1):
                for g in halves:
                    g.second(column, 0).wait_recv()
                    g.second(column, 2).start()
                    g.second(column, 1).wait_recv()
                    g.second(column, 3).start()
        elif step == 9:
            for g in halves:
                g.second(0, 2).wait_recv()
                g.second(0, 3).wait_recv()
        elif step == 11:
            for g in halves:
                g.second(2, 0).wait_recv()
                g.second(2, 2).start()
                g.second(2, 1).wait_recv()
                g.second(2, 3).start()
            for column in (-1, 1):
                for g in halves:
                    g.second(column, 2).wait_recv()
                    g.second(column, 3).wait_recv()
        elif step == 15:
            for g in halves:
                g.second(2, 2).wait_recv()
                g.second(2, 3).wait_recv()

    def body(step, carry):
        for number in (1, 2, 5, 9, 11, 15):
            @pl.when(step == number)
            def _():
                arrive(number)

        block = wrap(z, pick(step, [o[0] for o in ORDER])) * SIDE + wrap(
            y, pick(step, [o[1] for o in ORDER])
        )
        row0 = pl.multiple_of(block * TILE, TILE)
        q = qkvbuf[0, pl.ds(row0, TILE), :]
        k = qkvbuf[1]
        v = qkvbuf[2]
        d = dbuf[block]
        cot = nt(d, w_ref[...]).astype(jnp.bfloat16)
        scores = nt(q, k) * inv_root + bias[pl.ds(block, 1), :]
        top = jnp.max(scores, axis=-1, keepdims=True)
        expo = jnp.exp(scores - top)
        probs = expo * (1.0 / jnp.sum(expo, axis=-1, keepdims=True))
        probs_b = probs.astype(jnp.bfloat16)
        att = nn(probs_b, v).astype(jnp.bfloat16)
        delta = jnp.sum(
            cot.astype(jnp.float32) * att.astype(jnp.float32), axis=-1, keepdims=True
        )
        dscores = (probs * (nt(cot, v) - delta)).astype(jnp.bfloat16)
        grads_ref[0, pl.ds(row0, TILE), :] = (nn(dscores, k) * inv_root).astype(jnp.bfloat16)
        dkt[...] += tn(q, dscores)
        dvt[...] += tn(cot, probs_b)
        gw_ref[...] += tn(att, d)
        return carry

    lax.fori_loop(0, BLOCKS, body, 0)
    grads_ref[1] = (dkt[...].T * inv_root).astype(jnp.bfloat16)
    grads_ref[2] = dvt[...].T.astype(jnp.bfloat16)

    for copy in q_copies:
        copy.wait_send()
    for g in halves:
        for kind in range(4):
            g.first(kind).wait_send()
            for column in COLUMNS:
                g.second(column, kind).wait_send()


def body(qkv, tile_mask, d_out, w_out, momentum):
    worker_count = lax.axis_size("dp")
    tokens, head_size = qkv.shape[2], qkv.shape[4]
    width = d_out.shape[2]
    length = tokens * BLOCKS
    inv_root = 1.0 / math.sqrt(head_size)
    qkv_t = jnp.transpose(qkv[:, 0], (0, 2, 1, 3))
    vmem = pl.BlockSpec(memory_space=pltpu.VMEM)
    hbm = pl.BlockSpec(memory_space=pl.ANY)
    grads, weight_grad = pl.pallas_call(
        functools.partial(kernel, inv_root),
        out_shape=(
            jax.ShapeDtypeStruct((3, length, head_size), jnp.bfloat16),
            jax.ShapeDtypeStruct((head_size, width), jnp.float32),
        ),
        in_specs=[hbm, hbm, vmem, vmem],
        out_specs=(vmem, vmem),
        scratch_shapes=[
            pltpu.VMEM((3, length, head_size), jnp.bfloat16),
            pltpu.VMEM((BLOCKS, tokens, width), jnp.bfloat16),
            pltpu.VMEM((BLOCKS, length), jnp.float32),
            pltpu.VMEM((head_size, length), jnp.float32),
            pltpu.VMEM((head_size, length), jnp.float32),
            pltpu.SemaphoreType.DMA((BLOCKS - 1,)),
            pltpu.SemaphoreType.DMA((BLOCKS - 1,)),
            pltpu.SemaphoreType.DMA((40,)),
            pltpu.SemaphoreType.DMA((40,)),
            pltpu.SemaphoreType.DMA((2,)),
        ],
        compiler_params=pltpu.CompilerParams(
            collective_id=0, has_side_effects=True, vmem_limit_bytes=56 << 20
        ),
    )(qkv_t, d_out[0], w_out[0], tile_mask)
    head_grads = grads.reshape(3, 1, length, 1, head_size)
    grad_qkv = lax.all_to_all(head_grads, "seq", split_axis=2, concat_axis=3, tiled=True)
    worker_mom = 0.9 * momentum + 0.1 * weight_grad[None]
    worker_scale = jnp.mean(jnp.abs(worker_mom), axis=(1, 2), keepdims=True) + 1e-06
    sent = (worker_scale * jnp.tanh(worker_mom / worker_scale)).astype(jnp.bfloat16)
    worker_error = (worker_mom - sent.astype(jnp.float32))[None]
    received = lax.all_to_all(sent[None], "dp", split_axis=2, concat_axis=0, tiled=True)
    averaged = jnp.sum(received.astype(jnp.float32), axis=0) / worker_count
    server_scale = jnp.mean(jnp.abs(averaged), axis=(1, 2), keepdims=True) + 1e-06
    server_sent = (server_scale * jnp.tanh(averaged / server_scale)).astype(jnp.bfloat16)
    server_error = averaged - server_sent.astype(jnp.float32)
    synced_momentum = lax.all_gather(server_sent, "dp", axis=1, tiled=True)
    return (grad_qkv, synced_momentum, worker_error, server_error)


def solution(mesh):
    placed = (
        P(None, "dp", "seq", None, None),
        P(),
        P("dp", "seq", None),
        P("seq", None, None),
        P("seq", None, None),
    )
    return jax.shard_map(
        body,
        mesh=mesh,
        in_specs=placed,
        out_specs=(
            P(None, "dp", "seq", None, None),
            P("seq", None, None),
            P("dp", "seq", None, None),
            P("seq", "dp", None),
        ),
        check_vma=False,
    )
```

```python
import functools
import math

import jax
import jax.numpy as jnp
from jax import lax
from jax.experimental import pallas as pl
from jax.experimental.pallas import tpu as pltpu
from jax.sharding import PartitionSpec as P

HEADS = 16
GROUPS = 8
TILE = 128
SIDE = 4
BLOCKS = SIDE * SIDE
WORKERS = 8
HALF = TILE // 2
MESH = pl.DeviceIdType.MESH

ORDER = (
    (0, 0),
    (-1, 0), (1, 0), (0, -1), (0, 1),
    (-1, -1), (-1, 1), (1, -1), (1, 1),
    (2, 0), (0, 2),
    (2, -1), (2, 1), (-1, 2), (1, 2),
    (2, 2),
)
COLUMNS = (0, -1, 1, 2)


def wrap(position, offset):
    return lax.rem(position + (offset + SIDE), SIDE)


def pick(step, table):
    value = jnp.int32(table[0])
    for index, entry in enumerate(table):
        if index and entry != table[0]:
            value = jnp.where(step == index, jnp.int32(entry), value)
    return value


def nt(a, b):
    return lax.dot_general(a, b, (((1,), (1,)), ((), ())), preferred_element_type=jnp.float32)


def nn(a, b):
    return lax.dot_general(a, b, (((1,), (0,)), ((), ())), preferred_element_type=jnp.float32)


def tn(a, b):
    return lax.dot_general(a, b, (((0,), (0,)), ((), ())), preferred_element_type=jnp.float32)


class Gather:
    def __init__(self, buf, z, y, z_first, row0, sem0, send, recv):
        self.buf, self.z, self.y, self.z_first = buf, z, y, z_first
        self.row0, self.sem0, self.send, self.recv = row0, sem0, send, recv

    def block(self, a, b):
        dz, dy = (a, b) if self.z_first else (b, a)
        return wrap(self.z, dz) * SIDE + wrap(self.y, dy)

    def peer(self, a, b):
        return {"seq": self.block(a, b)}

    def copy(self, slot, block, lo, n, a, b):
        rows = self.buf.at[block, pl.ds(self.row0 + lo, n)]
        return pltpu.make_async_remote_copy(
            src_ref=rows,
            dst_ref=rows,
            send_sem=self.send.at[self.sem0 + slot],
            recv_sem=self.recv.at[self.sem0 + slot],
            device_id=self.peer(a, b),
            device_id_type=MESH,
        )

    def first(self, kind):
        if kind == 0:
            return self.copy(0, self.block(0, 0), 0, HALF, 1, 0)
        if kind == 1:
            return self.copy(1, self.block(0, 0), 0, HALF, -1, 0)
        if kind == 2:
            return self.copy(2, self.block(-1, 0), 0, HALF // 2, 1, 0)
        return self.copy(3, self.block(1, 0), HALF // 2, HALF // 2, -1, 0)

    def second(self, column, kind):
        slot = 4 + 4 * COLUMNS.index(column) + kind
        if kind == 0:
            return self.copy(slot, self.block(column, 0), 0, HALF, 0, 1)
        if kind == 1:
            return self.copy(slot, self.block(column, 0), 0, HALF, 0, -1)
        if kind == 2:
            return self.copy(slot, self.block(column, -1), 0, HALF // 2, 0, 1)
        return self.copy(slot, self.block(column, 1), HALF // 2, HALF // 2, 0, -1)


def kernel(
    inv_root,
    qkv_ref, dout_ref, w_hbm, mask_ref, mom_hbm,
    grads_ref, sync_ref, werr_ref, serr_ref,
    qkvbuf, dbuf, w_ref, mom_ref, bias, dqbuf, dkt, dvt, kvbuf, gw_ref,
    sentbuf, werrbuf, landed, syncbuf, serrbuf,
    q_send, q_recv, d_send, d_recv, g_send, g_recv, kv_send, kv_recv,
    m_send, m_recv, s_send, s_recv, local_sem,
):
    me = lax.axis_index("seq")
    z = me // SIDE
    y = lax.rem(me, SIDE)
    worker = lax.axis_index("dp")
    x = worker // 2
    core = lax.rem(worker, 2)
    width = dout_ref.shape[1]
    rows = sentbuf.shape[0] // WORKERS
    peers = [
        wrap(z, dz) * SIDE + wrap(y, dy)
        for dz in range(SIDE) for dy in range(SIDE) if (dz, dy) != (0, 0)
    ]
    workers = [
        wrap(x, dx) * 2 + lax.rem(core + dc, 2)
        for dx in (2, 1, -1, 0) for dc in range(2) if (dx, dc) != (0, 0)
    ]

    own_d = pltpu.make_async_copy(dout_ref, dbuf.at[me], local_sem.at[0])
    own_d.start()
    own_q = pltpu.make_async_copy(
        qkv_ref.at[:, me], qkvbuf.at[:, pl.ds(me * TILE, TILE)], local_sem.at[1]
    )
    own_q.start()
    own_w = pltpu.make_async_copy(w_hbm, w_ref, local_sem.at[2])
    own_w.start()
    own_m = pltpu.make_async_copy(mom_hbm, mom_ref, local_sem.at[3])
    own_m.start()

    barrier = pltpu.get_barrier_semaphore()
    for peer in peers:
        pl.semaphore_signal(barrier, inc=1, device_id={"seq": peer}, device_id_type=MESH)
    for peer in workers:
        pl.semaphore_signal(barrier, inc=1, device_id={"dp": peer}, device_id_type=MESH)
    pl.semaphore_wait(barrier, len(peers) + len(workers))

    q_copies = []
    for index, peer in enumerate(peers):
        copy = pltpu.make_async_remote_copy(
            src_ref=qkv_ref.at[:, peer],
            dst_ref=qkvbuf.at[:, pl.ds(me * TILE, TILE)],
            send_sem=q_send.at[index],
            recv_sem=q_recv.at[index],
            device_id={"seq": peer},
            device_id_type=MESH,
        )
        copy.start()
        q_copies.append(copy)

    halves = (
        Gather(dbuf, z, y, True, 0, 0, d_send, d_recv),
        Gather(dbuf, z, y, False, HALF, 20, d_send, d_recv),
    )
    own_d.wait()
    for g in halves:
        g.first(0).start()
        g.first(1).start()
    for g in halves:
        g.second(0, 0).start()
        g.second(0, 1).start()

    group = me // (HEADS // GROUPS)
    tiles = mask_ref[group]
    for j in range(BLOCKS):
        bias[:, j * TILE:(j + 1) * TILE] = jnp.broadcast_to(
            jnp.where(tiles[:, j:j + 1] > 0, 0.0, -jnp.inf), (BLOCKS, TILE)
        )
    dkt[...] = jnp.zeros_like(dkt)
    dvt[...] = jnp.zeros_like(dvt)
    gw_ref[...] = jnp.zeros_like(gw_ref)

    own_q.wait()
    own_w.wait()
    own_m.wait()
    for copy in q_copies:
        copy.wait_recv()

    def arrive(step):
        if step == 1:
            for g in halves:
                g.first(0).wait_recv()
                g.first(2).start()
                g.second(-1, 0).start()
                g.second(-1, 1).start()
            for g in halves:
                g.first(1).wait_recv()
                g.first(3).start()
                g.second(1, 0).start()
                g.second(1, 1).start()
            for g in halves:
                g.second(0, 0).wait_recv()
                g.second(0, 2).start()
                g.second(0, 1).wait_recv()
                g.second(0, 3).start()
        elif step == 2:
            for g in halves:
                g.first(2).wait_recv()
                g.first(3).wait_recv()
                g.second(2, 0).start()
                g.second(2, 1).start()
        elif step == 5:
            for column in (-1, 1):
                for g in halves:
                    g.second(column, 0).wait_recv()
                    g.second(column, 2).start()
                    g.second(column, 1).wait_recv()
                    g.second(column, 3).start()
        elif step == 9:
            for g in halves:
                g.second(0, 2).wait_recv()
                g.second(0, 3).wait_recv()
        elif step == 11:
            for g in halves:
                g.second(2, 0).wait_recv()
                g.second(2, 2).start()
                g.second(2, 1).wait_recv()
                g.second(2, 3).start()
            for column in (-1, 1):
                for g in halves:
                    g.second(column, 2).wait_recv()
                    g.second(column, 3).wait_recv()
        elif step == 15:
            for g in halves:
                g.second(2, 2).wait_recv()
                g.second(2, 3).wait_recv()

    def dq_copy(step, block):
        return pltpu.make_async_remote_copy(
            src_ref=dqbuf.at[pl.ds(pl.multiple_of(block * TILE, TILE), TILE)],
            dst_ref=grads_ref.at[0, me],
            send_sem=g_send.at[step],
            recv_sem=g_recv.at[step],
            device_id={"seq": block},
            device_id_type=MESH,
        )

    def block_of(step):
        return wrap(z, pick(step, [o[0] for o in ORDER])) * SIDE + wrap(
            y, pick(step, [o[1] for o in ORDER])
        )

    def body(step, carry):
        for number in (1, 2, 5, 9, 11, 15):
            @pl.when(step == number)
            def _():
                arrive(number)

        block = block_of(step)
        row0 = pl.multiple_of(block * TILE, TILE)
        q = qkvbuf[0, pl.ds(row0, TILE), :]
        k = qkvbuf[1]
        v = qkvbuf[2]
        d = dbuf[block]
        cot = nt(d, w_ref[...]).astype(jnp.bfloat16)
        scores = nt(q, k) * inv_root + bias[pl.ds(block, 1), :]
        top = jnp.max(scores, axis=-1, keepdims=True)
        expo = jnp.exp(scores - top)
        probs = expo * (1.0 / jnp.sum(expo, axis=-1, keepdims=True))
        probs_b = probs.astype(jnp.bfloat16)
        att = nn(probs_b, v).astype(jnp.bfloat16)
        delta = jnp.sum(
            cot.astype(jnp.float32) * att.astype(jnp.float32), axis=-1, keepdims=True
        )
        dscores = (probs * (nt(cot, v) - delta)).astype(jnp.bfloat16)
        dqbuf[pl.ds(row0, TILE), :] = (nn(dscores, k) * inv_root).astype(jnp.bfloat16)

        @pl.when(step > 0)
        def _():
            dq_copy(step, block).start()

        dkt[...] += tn(q, dscores)
        dvt[...] += tn(cot, probs_b)
        gw_ref[...] += tn(att, d)
        return carry

    lax.fori_loop(0, BLOCKS, body, 0)

    def moment(index, total):
        at = pl.ds(pl.multiple_of(index * rows, rows), rows)
        value = 0.9 * mom_ref[at, :] + 0.1 * gw_ref[at, :]
        mom_ref[at, :] = value
        return total + jnp.abs(value)

    total = lax.fori_loop(0, WORKERS, moment, jnp.zeros((rows, width), jnp.float32))
    scale = jnp.sum(total, axis=(0, 1), keepdims=True) / (rows * WORKERS * width) + 1e-06
    unscale = 1.0 / scale

    def compress(index, carry):
        at = pl.ds(pl.multiple_of(index * rows, rows), rows)
        value = mom_ref[at, :]
        code = (scale * jnp.tanh(value * unscale)).astype(jnp.bfloat16)
        sentbuf[at, :] = code
        werrbuf[at, :] = value - code.astype(jnp.float32)
        return carry

    lax.fori_loop(0, WORKERS, compress, 0)
    m_copies = []
    for index, peer in enumerate(workers):
        copy = pltpu.make_async_remote_copy(
            src_ref=sentbuf.at[pl.ds(pl.multiple_of(peer * rows, rows), rows)],
            dst_ref=landed.at[worker],
            send_sem=m_send.at[index],
            recv_sem=m_recv.at[index],
            device_id={"dp": peer},
            device_id_type=MESH,
        )
        copy.start()
        m_copies.append(copy)
    landed[worker] = sentbuf[pl.ds(pl.multiple_of(worker * rows, rows), rows), :]
    werr_out = pltpu.make_async_copy(werrbuf, werr_ref, local_sem.at[4])
    werr_out.start()

    kvbuf[0] = (dkt[...].T * inv_root).astype(jnp.bfloat16)
    kvbuf[1] = dvt[...].T.astype(jnp.bfloat16)
    kv_copies = []
    for index, peer in enumerate(peers):
        copy = pltpu.make_async_remote_copy(
            src_ref=kvbuf.at[:, pl.ds(peer * TILE, TILE)],
            dst_ref=grads_ref.at[pl.ds(1, 2), me],
            send_sem=kv_send.at[index],
            recv_sem=kv_recv.at[index],
            device_id={"seq": peer},
            device_id_type=MESH,
        )
        copy.start()
        kv_copies.append(copy)
    own_kv = pltpu.make_async_copy(
        kvbuf.at[:, pl.ds(me * TILE, TILE)], grads_ref.at[pl.ds(1, 2), me], local_sem.at[5]
    )
    own_kv.start()
    own_dq = pltpu.make_async_copy(
        dqbuf.at[pl.ds(me * TILE, TILE)], grads_ref.at[0, me], local_sem.at[6]
    )
    own_dq.start()

    for copy in m_copies:
        copy.wait_recv()
    average = landed[0].astype(jnp.float32)
    for index in range(1, WORKERS):
        average = average + landed[index].astype(jnp.float32)
    average = average / WORKERS
    server = jnp.sum(jnp.abs(average), axis=(0, 1), keepdims=True) / (rows * width) + 1e-06
    code = (server * jnp.tanh(average * (1.0 / server))).astype(jnp.bfloat16)
    syncbuf[...] = code
    serrbuf[...] = average - code.astype(jnp.float32)
    mine = sync_ref.at[pl.ds(pl.multiple_of(worker * rows, rows), rows)]
    s_copies = []
    for index, peer in enumerate(workers):
        copy = pltpu.make_async_remote_copy(
            src_ref=syncbuf,
            dst_ref=mine,
            send_sem=s_send.at[index],
            recv_sem=s_recv.at[index],
            device_id={"dp": peer},
            device_id_type=MESH,
        )
        copy.start()
        s_copies.append(copy)
    own_s = pltpu.make_async_copy(syncbuf, mine, local_sem.at[7])
    own_s.start()
    serr_out = pltpu.make_async_copy(serrbuf, serr_ref, local_sem.at[8])
    serr_out.start()

    for copy in q_copies:
        copy.wait_send()
    for g in halves:
        for kind in range(4):
            g.first(kind).wait_send()
            for column in COLUMNS:
                g.second(column, kind).wait_send()
    for copy in m_copies:
        copy.wait_send()

    def drain(step, carry):
        dq_copy(step, block_of(step)).wait()
        return carry

    lax.fori_loop(1, BLOCKS, drain, 0)
    for copy in kv_copies + s_copies:
        copy.wait()
    for copy in (own_kv, own_dq, own_s, werr_out, serr_out):
        copy.wait()


def body(qkv, tile_mask, d_out, w_out, momentum):
    tokens, head_size = qkv.shape[2], qkv.shape[4]
    width = d_out.shape[2]
    length = tokens * BLOCKS
    inv_root = 1.0 / math.sqrt(head_size)
    rows = head_size // WORKERS
    qkv_t = jnp.transpose(qkv[:, 0], (0, 2, 1, 3))
    vmem = pl.BlockSpec(memory_space=pltpu.VMEM)
    hbm = pl.BlockSpec(memory_space=pl.ANY)
    dma = pltpu.SemaphoreType.DMA
    grads, synced, worker_error, server_error = pl.pallas_call(
        functools.partial(kernel, inv_root),
        out_shape=(
            jax.ShapeDtypeStruct((3, HEADS, tokens, head_size), jnp.bfloat16),
            jax.ShapeDtypeStruct((head_size, width), jnp.bfloat16),
            jax.ShapeDtypeStruct((head_size, width), jnp.float32),
            jax.ShapeDtypeStruct((rows, width), jnp.float32),
        ),
        in_specs=[hbm, hbm, hbm, vmem, hbm],
        out_specs=(hbm, hbm, hbm, hbm),
        scratch_shapes=[
            pltpu.VMEM((3, length, head_size), jnp.bfloat16),
            pltpu.VMEM((BLOCKS, tokens, width), jnp.bfloat16),
            pltpu.VMEM((head_size, width), jnp.bfloat16),
            pltpu.VMEM((head_size, width), jnp.float32),
            pltpu.VMEM((BLOCKS, length), jnp.float32),
            pltpu.VMEM((length, head_size), jnp.bfloat16),
            pltpu.VMEM((head_size, length), jnp.float32),
            pltpu.VMEM((head_size, length), jnp.float32),
            pltpu.VMEM((2, length, head_size), jnp.bfloat16),
            pltpu.VMEM((head_size, width), jnp.float32),
            pltpu.VMEM((head_size, width), jnp.bfloat16),
            pltpu.VMEM((head_size, width), jnp.float32),
            pltpu.VMEM((WORKERS, rows, width), jnp.bfloat16),
            pltpu.VMEM((rows, width), jnp.bfloat16),
            pltpu.VMEM((rows, width), jnp.float32),
            dma((BLOCKS - 1,)), dma((BLOCKS - 1,)),
            dma((40,)), dma((40,)),
            dma((BLOCKS,)), dma((BLOCKS,)),
            dma((BLOCKS - 1,)), dma((BLOCKS - 1,)),
            dma((WORKERS - 1,)), dma((WORKERS - 1,)),
            dma((WORKERS - 1,)), dma((WORKERS - 1,)),
            dma((9,)),
        ],
        compiler_params=pltpu.CompilerParams(
            collective_id=0, has_side_effects=True, vmem_limit_bytes=56 << 20
        ),
    )(qkv_t, d_out[0], w_out[0], tile_mask, momentum[0])
    grad_qkv = jnp.transpose(grads, (0, 2, 1, 3))[:, None]
    return (grad_qkv, synced[None], worker_error[None, None], server_error[None])


def solution(mesh):
    placed = (
        P(None, "dp", "seq", None, None),
        P(),
        P("dp", "seq", None),
        P("seq", None, None),
        P("seq", None, None),
    )
    return jax.shard_map(
        body,
        mesh=mesh,
        in_specs=placed,
        out_specs=(
            P(None, "dp", "seq", None, None),
            P("seq", None, None),
            P("dp", "seq", None, None),
            P("seq", "dp", None),
        ),
        check_vma=False,
    )
```

```python
import functools
import math

import jax
import jax.numpy as jnp
from jax import lax
from jax.experimental import pallas as pl
from jax.experimental.pallas import tpu as pltpu
from jax.sharding import PartitionSpec as P

HEADS = 16
GROUPS = 8
TILE = 128
SIDE = 4
BLOCKS = SIDE * SIDE
WORKERS = 8
HALF = TILE // 2
PART = HALF // 2
MESH = pl.DeviceIdType.MESH

ORDER = (
    (0, 0), (0, 1), (0, 2), (0, 3),
    (-1, 0), (-1, 1), (1, 0), (1, 1),
    (2, 0), (2, 1),
    (-1, 2), (-1, 3), (1, 2), (1, 3),
    (2, 2), (2, 3),
)
OFFSETS = (0, -1, 1, 2)


def wrap(position, offset):
    return lax.rem(position + (offset + SIDE), SIDE)


def pick(step, table):
    value = jnp.int32(table[0])
    for index, entry in enumerate(table):
        if index and entry != table[0]:
            value = jnp.where(step == index, jnp.int32(entry), value)
    return value


def nt(a, b):
    return lax.dot_general(a, b, (((1,), (1,)), ((), ())), preferred_element_type=jnp.float32)


def nn(a, b):
    return lax.dot_general(a, b, (((1,), (0,)), ((), ())), preferred_element_type=jnp.float32)


def tn(a, b):
    return lax.dot_general(a, b, (((0,), (0,)), ((), ())), preferred_element_type=jnp.float32)


class Gather:
    def __init__(self, buf, z, columns, row0, send, recv):
        self.buf, self.z, self.columns, self.row0 = buf, z, columns, row0
        self.send, self.recv = send, recv

    def block(self, dz, column):
        return wrap(self.z, dz) * SIDE + self.columns[column]

    def copy(self, slot, block, lo, n, dz, column):
        rows = self.buf.at[block, pl.ds(pl.multiple_of(self.row0 + lo, PART // 2), n)]
        return pltpu.make_async_remote_copy(
            src_ref=rows,
            dst_ref=rows,
            send_sem=self.send.at[slot],
            recv_sem=self.recv.at[slot],
            device_id={"seq": self.block(dz, column)},
            device_id_type=MESH,
        )

    def ring(self, slot, column, kind, lo):
        if kind == 0:
            return self.copy(slot, self.block(0, column), lo, PART, 1, 0)
        if kind == 1:
            return self.copy(slot, self.block(0, column), lo, PART, -1, 0)
        if kind == 2:
            return self.copy(slot, self.block(-1, column), lo, PART // 2, 1, 0)
        return self.copy(slot, self.block(1, column), lo + PART // 2, PART // 2, -1, 0)

    def az(self, column, kind):
        return self.ring(column * 4 + kind, column, kind, 0)

    def ay(self, dz, column):
        slot = 8 + OFFSETS.index(dz) * 2 + column
        return self.copy(slot, self.block(dz, column), 0, PART, 0, 2)

    def by(self, column):
        return self.copy(16 + column, self.block(0, column), PART, PART, 0, 2)

    def bz(self, column, kind):
        return self.ring(18 + column * 4 + kind, column, kind, PART)

    def every(self):
        copies = [self.az(c, kind) for c in range(2) for kind in range(4)]
        copies += [self.ay(dz, c) for dz in OFFSETS for c in range(2)]
        copies += [self.by(c) for c in range(2)]
        return copies + [self.bz(c, kind) for c in range(4) for kind in range(4)]


def kernel(
    inv_root,
    qkv_ref, dout_ref, w_hbm, mask_ref, mom_hbm,
    grads_ref, sync_ref, werr_ref, serr_ref,
    qkvbuf, dbuf, w_ref, mom_ref, bias, dqbuf, dkt, dvt, kvbuf, gw_ref,
    sentbuf, werrbuf, landed, syncbuf, serrbuf, gwout, gwin,
    q_send, q_recv, d_send, d_recv, f_send, f_recv, i_send, i_recv,
    g_send, g_recv, kv_send, kv_recv, x_send, x_recv,
    m_send, m_recv, s_send, s_recv, local_sem,
):
    me = lax.axis_index("seq")
    z = me // SIDE
    y = lax.rem(me, SIDE)
    worker = lax.axis_index("dp")
    x = worker // 2
    core = lax.rem(worker, 2)
    width = dout_ref.shape[1]
    rows = sentbuf.shape[0] // WORKERS

    side = y // 2
    home = core == side
    away = core != side
    columns = (y, 3 - y, y + 1 - 2 * lax.rem(y, 2), 2 - y + 2 * lax.rem(y, 2))
    other = x * 2 + 1 - core
    partner = z * SIDE + 3 - y
    head = jnp.where(home, me, partner)
    swap = {"dp": other, "seq": partner}
    slot_of_job = lax.rem(y, 2) * 2 + core

    own_d = pltpu.make_async_copy(dout_ref, dbuf.at[me], local_sem.at[0])
    own_q = pltpu.make_async_copy(
        qkv_ref.at[:, me], qkvbuf.at[:, pl.ds(me * TILE, TILE)], local_sem.at[1]
    )
    own_w = pltpu.make_async_copy(w_hbm, w_ref, local_sem.at[2])
    own_m = pltpu.make_async_copy(mom_hbm, mom_ref, local_sem.at[3])

    @pl.when(home)
    def _():
        own_d.start()
        own_q.start()
        own_w.start()

    own_m.start()

    workers = [
        wrap(x, dx) * 2 + lax.rem(core + dc, 2)
        for dx in (2, 1, -1, 0) for dc in range(2) if (dx, dc) != (0, 0)
    ]
    plane = [
        (x * 2 + lax.rem(core + dc, 2), wrap(z, dz) * SIDE + wrap(y, dy))
        for dc in range(2) for dz in range(SIDE) for dy in range(SIDE) if (dc, dz, dy) != (0, 0, 0)
    ]
    barrier = pltpu.get_barrier_semaphore()
    for dp, seq in plane:
        pl.semaphore_signal(
            barrier, inc=1, device_id={"dp": dp, "seq": seq}, device_id_type=MESH
        )
    for peer in workers[:-1]:
        pl.semaphore_signal(barrier, inc=1, device_id={"dp": peer}, device_id_type=MESH)
    pl.semaphore_wait(barrier, len(plane) + len(workers) - 1)

    starts = []
    for h in range(2):
        at = pl.ds(h * HALF, HALF)
        copy = pltpu.make_async_remote_copy(
            src_ref=dout_ref.at[at],
            dst_ref=dbuf.at[me, at],
            send_sem=i_send.at[h],
            recv_sem=i_recv.at[jnp.where(home, h, 2)],
            device_id={
                "dp": jnp.where(home, other, x * 2 + h),
                "seq": jnp.where(home, me, partner),
            },
            device_id_type=MESH,
        )
        copy.start()
        starts.append(copy)

    def landing(slot):
        at = pl.ds(0, HALF)
        return pltpu.make_async_remote_copy(
            src_ref=dout_ref.at[at],
            dst_ref=dbuf.at[me, at],
            send_sem=i_send.at[0],
            recv_sem=i_recv.at[slot],
            device_id=swap,
            device_id_type=MESH,
        )

    w_copy = pltpu.make_async_remote_copy(
        src_ref=w_hbm, dst_ref=w_ref, send_sem=x_send.at[0], recv_sem=x_recv.at[0],
        device_id=swap, device_id_type=MESH,
    )
    pl.when(away)(w_copy.start)

    def q_copy(dz, u, c, recv):
        z2, y2 = wrap(z, dz), 2 * core + u
        theirs = z2 * SIDE + jnp.where(core == c, y2, 3 - y2)
        return pltpu.make_async_remote_copy(
            src_ref=qkv_ref.at[:, theirs],
            dst_ref=qkvbuf.at[:, pl.ds(me * TILE, TILE)],
            send_sem=q_send.at[dz * 4 + u * 2 + c],
            recv_sem=q_recv.at[recv],
            device_id={"dp": x * 2 + c, "seq": z2 * SIDE + y2},
            device_id_type=MESH,
        )

    def q_mine(dz, u, c):
        return (2 * core + u == y) & (core == c) if dz == 0 else None

    def unless(mine, action):
        if mine is None:
            action()
        else:
            pl.when(jnp.logical_not(mine))(action)

    q_keys = [(dz, u, c) for dz in range(SIDE) for u in range(2) for c in range(2)]
    for key in q_keys:
        unless(q_mine(*key), q_copy(*key, key[0] * 4 + y).start)

    gather = Gather(dbuf, z, columns, core * HALF, d_send, d_recv)

    def launch(column):
        gather.by(column).start()
        gather.az(column, 0).start()
        gather.az(column, 1).start()
        gather.ay(0, column).start()
        gather.bz(column, 0).start()
        gather.bz(column, 1).start()

    def block_of(step):
        column = pick(step, [o[1] for o in ORDER])
        base = jnp.where(column < 2, columns[0], columns[2])
        return wrap(z, pick(step, [o[0] for o in ORDER])) * SIDE + jnp.where(
            lax.rem(column, 2) == 0, base, 3 - base
        )

    def forward(step, block):
        at = dbuf.at[block, pl.ds(pl.multiple_of(core * HALF, HALF), HALF)]
        return pltpu.make_async_remote_copy(
            src_ref=at, dst_ref=at, send_sem=f_send.at[step], recv_sem=f_recv.at[step],
            device_id={"dp": other}, device_id_type=MESH,
        )

    def pass_on(dz, column):
        forward(ORDER.index((dz, column)), gather.block(dz, column)).start()

    pl.when(home)(own_d.wait)
    pl.when(away)(landing(core).wait_recv)
    launch(0)
    landing(2).wait_recv()
    launch(1)
    pass_on(0, 1)

    tiles = mask_ref[head // (HEADS // GROUPS)]
    for j in range(BLOCKS):
        bias[:, j * TILE:(j + 1) * TILE] = jnp.broadcast_to(
            jnp.where(tiles[:, j:j + 1] > 0, 0.0, -jnp.inf), (BLOCKS, TILE)
        )
    dkt[...] = jnp.zeros_like(dkt)
    dvt[...] = jnp.zeros_like(dvt)
    gw_ref[...] = jnp.zeros_like(gw_ref)

    for column in range(2):
        gather.az(column, 0).wait_recv()
        gather.az(column, 2).start()
        gather.ay(-1, column).start()
        gather.az(column, 1).wait_recv()
        gather.az(column, 3).start()
        gather.ay(1, column).start()
    for column in range(2):
        gather.by(column).wait_recv()
        gather.bz(column + 2, 0).start()
        gather.bz(column + 2, 1).start()

    own_m.wait()
    pl.when(away)(landing(1 - core).wait_recv)
    pl.when(home)(own_q.wait)
    pl.when(home)(own_w.wait)
    pl.when(away)(w_copy.wait_recv)
    for dz in range(SIDE):
        for source in range(SIDE):
            unless((y == source) & home if dz == 0 else None,
                   q_copy(dz, 0, 0, dz * 4 + source).wait_recv)

    def arrive(step):
        if step == 2:
            for column in range(2):
                gather.ay(0, column).wait_recv()
                pass_on(0, column + 2)
        elif step == 4:
            for column in range(2):
                gather.az(column, 2).wait_recv()
                gather.az(column, 3).wait_recv()
                gather.ay(2, column).start()
            for column in range(2):
                gather.bz(column, 0).wait_recv()
                gather.bz(column, 2).start()
                pass_on(-1, column)
                gather.bz(column, 1).wait_recv()
                gather.bz(column, 3).start()
                pass_on(1, column)
        elif step == 8:
            for column in range(2):
                gather.bz(column, 2).wait_recv()
                gather.bz(column, 3).wait_recv()
                pass_on(2, column)
            for column in range(2, 4):
                gather.bz(column, 0).wait_recv()
                gather.bz(column, 2).start()
                gather.bz(column, 1).wait_recv()
                gather.bz(column, 3).start()
        elif step == 10:
            for column in range(2):
                gather.ay(-1, column).wait_recv()
                pass_on(-1, column + 2)
        elif step == 12:
            for column in range(2):
                gather.ay(1, column).wait_recv()
                pass_on(1, column + 2)
        elif step == 14:
            for column in range(2):
                gather.bz(column + 2, 2).wait_recv()
                gather.bz(column + 2, 3).wait_recv()
                gather.ay(2, column).wait_recv()
                pass_on(2, column + 2)

    def dq_copy(step, block, recv):
        return pltpu.make_async_remote_copy(
            src_ref=dqbuf.at[pl.ds(pl.multiple_of(block * TILE, TILE), TILE)],
            dst_ref=grads_ref.at[0, head],
            send_sem=g_send.at[step],
            recv_sem=g_recv.at[recv],
            device_id={"dp": x * 2 + side, "seq": block},
            device_id_type=MESH,
        )

    def body(step, carry):
        for number in (2, 4, 8, 10, 12, 14):
            @pl.when(step == number)
            def _():
                arrive(number)

        block = block_of(step)
        pl.when(step > 0)(forward(step, block).wait_recv)
        row0 = pl.multiple_of(block * TILE, TILE)
        q = qkvbuf[0, pl.ds(row0, TILE), :]
        k = qkvbuf[1]
        v = qkvbuf[2]
        d = dbuf[block]
        cot = nt(d, w_ref[...]).astype(jnp.bfloat16)
        scores = nt(q, k) * inv_root + bias[pl.ds(block, 1), :]
        top = jnp.max(scores, axis=-1, keepdims=True)
        expo = jnp.exp(scores - top)
        probs = expo * (1.0 / jnp.sum(expo, axis=-1, keepdims=True))
        probs_b = probs.astype(jnp.bfloat16)
        att = nn(probs_b, v).astype(jnp.bfloat16)
        delta = jnp.sum(
            cot.astype(jnp.float32) * att.astype(jnp.float32), axis=-1, keepdims=True
        )
        dscores = (probs * (nt(cot, v) - delta)).astype(jnp.bfloat16)
        dqbuf[pl.ds(row0, TILE), :] = (nn(dscores, k) * inv_root).astype(jnp.bfloat16)

        hop = lax.rem(pick(step, [o[0] for o in ORDER]) + SIDE, SIDE)
        pl.when((step > 0) | away)(dq_copy(step, block, hop * 4 + slot_of_job).start)

        dkt[...] += tn(q, dscores)
        dvt[...] += tn(cot, probs_b)
        gw_ref[...] += tn(att, d)
        return carry

    lax.fori_loop(0, BLOCKS, body, 0)

    gw_copy = pltpu.make_async_remote_copy(
        src_ref=gwout, dst_ref=gwin, send_sem=x_send.at[1], recv_sem=x_recv.at[1],
        device_id=swap, device_id_type=MESH,
    )

    @pl.when(away)
    def _():
        gwout[...] = gw_ref[...].astype(jnp.bfloat16)
        gw_copy.start()

    kvbuf[0] = (dkt[...].T * inv_root).astype(jnp.bfloat16)
    kvbuf[1] = dvt[...].T.astype(jnp.bfloat16)

    def kv_copy(dz, target, recv):
        block = wrap(z, dz) * SIDE + target
        return pltpu.make_async_remote_copy(
            src_ref=kvbuf.at[:, pl.ds(pl.multiple_of(block * TILE, TILE), TILE)],
            dst_ref=grads_ref.at[pl.ds(1, 2), head],
            send_sem=kv_send.at[dz * 4 + target],
            recv_sem=kv_recv.at[recv],
            device_id={"dp": x * 2 + side, "seq": block},
            device_id_type=MESH,
        )

    def kv_mine(dz, target):
        return (y == target) & home if dz == 0 else None

    kv_keys = [(dz, target) for dz in (2, 1, 3, 0) for target in range(SIDE)]
    for key in kv_keys:
        unless(kv_mine(*key), kv_copy(*key, key[0] * 4 + slot_of_job).start)
    own_kv = pltpu.make_async_copy(
        kvbuf.at[:, pl.ds(pl.multiple_of(me * TILE, TILE), TILE)],
        grads_ref.at[pl.ds(1, 2), me],
        local_sem.at[5],
    )
    own_dq = pltpu.make_async_copy(
        dqbuf.at[pl.ds(pl.multiple_of(me * TILE, TILE), TILE)], grads_ref.at[0, me], local_sem.at[6]
    )

    @pl.when(home)
    def _():
        own_kv.start()
        own_dq.start()

    @pl.when(away)
    def _():
        gw_copy.wait_recv()
        gw_ref[...] = gwin[...].astype(jnp.float32)

    def moment(index, total):
        at = pl.ds(pl.multiple_of(index * rows, rows), rows)
        value = 0.9 * mom_ref[at, :] + 0.1 * gw_ref[at, :]
        mom_ref[at, :] = value
        return total + jnp.abs(value)

    total = lax.fori_loop(0, WORKERS, moment, jnp.zeros((rows, width), jnp.float32))
    scale = jnp.sum(total, axis=(0, 1), keepdims=True) / (rows * WORKERS * width) + 1e-06
    unscale = 1.0 / scale

    def compress(index, carry):
        at = pl.ds(pl.multiple_of(index * rows, rows), rows)
        value = mom_ref[at, :]
        code = (scale * jnp.tanh(value * unscale)).astype(jnp.bfloat16)
        sentbuf[at, :] = code
        werrbuf[at, :] = value - code.astype(jnp.float32)
        return carry

    lax.fori_loop(0, WORKERS, compress, 0)
    m_copies = []
    for index, peer in enumerate(workers):
        copy = pltpu.make_async_remote_copy(
            src_ref=sentbuf.at[pl.ds(pl.multiple_of(peer * rows, rows), rows)],
            dst_ref=landed.at[worker],
            send_sem=m_send.at[index],
            recv_sem=m_recv.at[index],
            device_id={"dp": peer},
            device_id_type=MESH,
        )
        copy.start()
        m_copies.append(copy)
    landed[worker] = sentbuf[pl.ds(pl.multiple_of(worker * rows, rows), rows), :]
    werr_out = pltpu.make_async_copy(werrbuf, werr_ref, local_sem.at[4])
    werr_out.start()

    for copy in m_copies:
        copy.wait_recv()
    average = landed[0].astype(jnp.float32)
    for index in range(1, WORKERS):
        average = average + landed[index].astype(jnp.float32)
    average = average / WORKERS
    server = jnp.sum(jnp.abs(average), axis=(0, 1), keepdims=True) / (rows * width) + 1e-06
    code = (server * jnp.tanh(average * (1.0 / server))).astype(jnp.bfloat16)
    syncbuf[...] = code
    serrbuf[...] = average - code.astype(jnp.float32)
    mine = sync_ref.at[pl.ds(pl.multiple_of(worker * rows, rows), rows)]
    s_copies = []
    for index, peer in enumerate(workers):
        copy = pltpu.make_async_remote_copy(
            src_ref=syncbuf,
            dst_ref=mine,
            send_sem=s_send.at[index],
            recv_sem=s_recv.at[index],
            device_id={"dp": peer},
            device_id_type=MESH,
        )
        copy.start()
        s_copies.append(copy)
    own_s = pltpu.make_async_copy(syncbuf, mine, local_sem.at[7])
    own_s.start()
    serr_out = pltpu.make_async_copy(serrbuf, serr_ref, local_sem.at[8])
    serr_out.start()

    for key in q_keys:
        unless(q_mine(*key), q_copy(*key, 0).wait_send)
    for copy in gather.every() + starts + m_copies:
        copy.wait_send()
    for copy in s_copies:
        copy.wait()

    @pl.when(away)
    def _():
        w_copy.wait_send()
        gw_copy.wait_send()

    for step in range(1, BLOCKS):
        forward(step, me).wait_send()

    for step in range(BLOCKS):
        unless(home if step == 0 else None, dq_copy(step, me, 0).wait_send)
    for key in kv_keys:
        unless(kv_mine(*key), kv_copy(*key, 0).wait_send)
    for slot in range(BLOCKS):
        mine = home & (slot_of_job == slot) if slot < 4 else None
        unless(mine, dq_copy(0, me, slot).wait_recv)
        unless(mine, kv_copy(0, 0, slot).wait_recv)

    @pl.when(home)
    def _():
        own_kv.wait()
        own_dq.wait()

    for copy in (own_s, werr_out, serr_out):
        copy.wait()


def body(qkv, tile_mask, d_out, w_out, momentum):
    tokens, head_size = qkv.shape[2], qkv.shape[4]
    width = d_out.shape[2]
    length = tokens * BLOCKS
    inv_root = 1.0 / math.sqrt(head_size)
    rows = head_size // WORKERS
    qkv_t = jnp.transpose(qkv[:, 0], (0, 2, 1, 3))
    vmem = pl.BlockSpec(memory_space=pltpu.VMEM)
    hbm = pl.BlockSpec(memory_space=pl.ANY)
    dma = pltpu.SemaphoreType.DMA
    grads, synced, worker_error, server_error = pl.pallas_call(
        functools.partial(kernel, inv_root),
        out_shape=(
            jax.ShapeDtypeStruct((3, HEADS, tokens, head_size), jnp.bfloat16),
            jax.ShapeDtypeStruct((head_size, width), jnp.bfloat16),
            jax.ShapeDtypeStruct((head_size, width), jnp.float32),
            jax.ShapeDtypeStruct((rows, width), jnp.float32),
        ),
        in_specs=[hbm, hbm, hbm, vmem, hbm],
        out_specs=(hbm, hbm, hbm, hbm),
        scratch_shapes=[
            pltpu.VMEM((3, length, head_size), jnp.bfloat16),
            pltpu.VMEM((BLOCKS, tokens, width), jnp.bfloat16),
            pltpu.VMEM((head_size, width), jnp.bfloat16),
            pltpu.VMEM((head_size, width), jnp.float32),
            pltpu.VMEM((BLOCKS, length), jnp.float32),
            pltpu.VMEM((length, head_size), jnp.bfloat16),
            pltpu.VMEM((head_size, length), jnp.float32),
            pltpu.VMEM((head_size, length), jnp.float32),
            pltpu.VMEM((2, length, head_size), jnp.bfloat16),
            pltpu.VMEM((head_size, width), jnp.float32),
            pltpu.VMEM((head_size, width), jnp.bfloat16),
            pltpu.VMEM((head_size, width), jnp.float32),
            pltpu.VMEM((WORKERS, rows, width), jnp.bfloat16),
            pltpu.VMEM((rows, width), jnp.bfloat16),
            pltpu.VMEM((rows, width), jnp.float32),
            pltpu.VMEM((head_size, width), jnp.bfloat16),
            pltpu.VMEM((head_size, width), jnp.bfloat16),
            dma((BLOCKS,)), dma((BLOCKS,)),
            dma((34,)), dma((34,)),
            dma((BLOCKS,)), dma((BLOCKS,)),
            dma((2,)), dma((3,)),
            dma((BLOCKS,)), dma((BLOCKS,)),
            dma((BLOCKS,)), dma((BLOCKS,)),
            dma((2,)), dma((2,)),
            dma((WORKERS - 1,)), dma((WORKERS - 1,)),
            dma((WORKERS - 1,)), dma((WORKERS - 1,)),
            dma((9,)),
        ],
        compiler_params=pltpu.CompilerParams(
            collective_id=0, has_side_effects=True, vmem_limit_bytes=56 << 20
        ),
    )(qkv_t, d_out[0], w_out[0], tile_mask, momentum[0])
    grad_qkv = jnp.transpose(grads, (0, 2, 1, 3))[:, None]
    return (grad_qkv, synced[None], worker_error[None, None], server_error[None])


def solution(mesh):
    placed = (
        P(None, "dp", "seq", None, None),
        P(),
        P("dp", "seq", None),
        P("seq", None, None),
        P("seq", None, None),
    )
    return jax.shard_map(
        body,
        mesh=mesh,
        in_specs=placed,
        out_specs=(
            P(None, "dp", "seq", None, None),
            P("seq", None, None),
            P("dp", "seq", None, None),
            P("seq", "dp", None),
        ),
        check_vma=False,
    )
```

```python
import functools
import math

import jax
import jax.numpy as jnp
from jax import lax
from jax.experimental import pallas as pl
from jax.experimental.pallas import tpu as pltpu
from jax.sharding import PartitionSpec as P

HEADS = 16
GROUPS = 8
TILE = 128
SIDE = 4
BLOCKS = SIDE * SIDE
WORKERS = 8
HALF = TILE // 2
PART = HALF // 2
MESH = pl.DeviceIdType.MESH

ORDER = (
    (0, 0), (0, 1), (0, 2), (0, 3),
    (-1, 0), (-1, 1), (1, 0), (1, 1),
    (2, 0), (2, 1),
    (-1, 2), (-1, 3), (1, 2), (1, 3),
    (2, 2), (2, 3),
)
OFFSETS = (0, -1, 1, 2)


def wrap(position, offset):
    return lax.rem(position + (offset + SIDE), SIDE)


def pick(step, table):
    value = jnp.int32(table[0])
    for index, entry in enumerate(table):
        if index and entry != table[0]:
            value = jnp.where(step == index, jnp.int32(entry), value)
    return value


def nt(a, b):
    return lax.dot_general(a, b, (((1,), (1,)), ((), ())), preferred_element_type=jnp.float32)


def nn(a, b):
    return lax.dot_general(a, b, (((1,), (0,)), ((), ())), preferred_element_type=jnp.float32)


def tn(a, b):
    return lax.dot_general(a, b, (((0,), (0,)), ((), ())), preferred_element_type=jnp.float32)


class Gather:
    def __init__(self, buf, z, columns, row0, send, recv):
        self.buf, self.z, self.columns, self.row0 = buf, z, columns, row0
        self.send, self.recv = send, recv

    def block(self, dz, column):
        return wrap(self.z, dz) * SIDE + self.columns[column]

    def copy(self, slot, block, lo, n, dz, column):
        rows = self.buf.at[block, pl.ds(pl.multiple_of(self.row0 + lo, PART // 2), n)]
        return pltpu.make_async_remote_copy(
            src_ref=rows,
            dst_ref=rows,
            send_sem=self.send.at[slot],
            recv_sem=self.recv.at[slot],
            device_id={"seq": self.block(dz, column)},
            device_id_type=MESH,
        )

    def ring(self, slot, column, kind, lo):
        if kind == 0:
            return self.copy(slot, self.block(0, column), lo, PART, 1, 0)
        if kind == 1:
            return self.copy(slot, self.block(0, column), lo, PART, -1, 0)
        if kind == 2:
            return self.copy(slot, self.block(-1, column), lo, PART // 2, 1, 0)
        return self.copy(slot, self.block(1, column), lo + PART // 2, PART // 2, -1, 0)

    def az(self, column, kind):
        return self.ring(column * 4 + kind, column, kind, 0)

    def ay(self, dz, column):
        slot = 8 + OFFSETS.index(dz) * 2 + column
        return self.copy(slot, self.block(dz, column), 0, PART, 0, 2)

    def by(self, column):
        return self.copy(16 + column, self.block(0, column), PART, PART, 0, 2)

    def bz(self, column, kind):
        return self.ring(18 + column * 4 + kind, column, kind, PART)

    def every(self):
        copies = [self.az(c, kind) for c in range(2) for kind in range(4)]
        copies += [self.ay(dz, c) for dz in OFFSETS for c in range(2)]
        copies += [self.by(c) for c in range(2)]
        return copies + [self.bz(c, kind) for c in range(4) for kind in range(4)]


def kernel(
    inv_root,
    qkv_ref, dout_ref, w_hbm, mask_ref, mom_hbm,
    grads_ref, sync_ref, werr_ref, serr_ref,
    qkvbuf, dbuf, w_ref, mom_ref, bias, dqbuf, dkt, dvt, kvbuf, gw_ref,
    sentbuf, werrbuf, landed, parts, sums, syncbuf, serrbuf, gwout, gwin, jobmom,
    q_send, q_recv, d_send, d_recv, f_send, f_recv, i_send, i_recv,
    g_send, g_recv, kv_send, kv_recv, x_send, x_recv,
    m_send, m_recv, p_send, p_recv, s_send, s_recv, local_sem,
):
    me = lax.axis_index("seq")
    z = me // SIDE
    y = lax.rem(me, SIDE)
    worker = lax.axis_index("dp")
    x = worker // 2
    core = lax.rem(worker, 2)
    width = dout_ref.shape[1]
    rows = sentbuf.shape[0] // WORKERS

    side = y // 2
    home = core == side
    away = core != side
    columns = (y, 3 - y, y + 1 - 2 * lax.rem(y, 2), 2 - y + 2 * lax.rem(y, 2))
    other = x * 2 + 1 - core
    partner = z * SIDE + 3 - y
    head = jnp.where(home, me, partner)
    swap = {"dp": other, "seq": partner}
    slot_of_job = lax.rem(y, 2) * 2 + core

    own_d = pltpu.make_async_copy(dout_ref, dbuf.at[me], local_sem.at[0])
    own_q = pltpu.make_async_copy(
        qkv_ref.at[:, me], qkvbuf.at[:, pl.ds(me * TILE, TILE)], local_sem.at[1]
    )
    own_w = pltpu.make_async_copy(w_hbm, w_ref, local_sem.at[2])
    own_m = pltpu.make_async_copy(mom_hbm, mom_ref, local_sem.at[3])
    home_m = pltpu.make_async_copy(mom_hbm, jobmom, local_sem.at[3])

    @pl.when(home)
    def _():
        own_d.start()
        own_q.start()
        own_w.start()
        home_m.start()

    pl.when(away)(own_m.start)

    workers = [
        wrap(x, dx) * 2 + lax.rem(core + dc, 2)
        for dx in (2, 1, -1, 0) for dc in range(2) if (dx, dc) != (0, 0)
    ]
    plane = [
        (x * 2 + lax.rem(core + dc, 2), wrap(z, dz) * SIDE + wrap(y, dy))
        for dc in range(2) for dz in range(SIDE) for dy in range(SIDE) if (dc, dz, dy) != (0, 0, 0)
    ]
    barrier = pltpu.get_barrier_semaphore()
    for dp, seq in plane:
        pl.semaphore_signal(
            barrier, inc=1, device_id={"dp": dp, "seq": seq}, device_id_type=MESH
        )
    for peer in workers[:-1]:
        pl.semaphore_signal(barrier, inc=1, device_id={"dp": peer}, device_id_type=MESH)
    pl.semaphore_wait(barrier, len(plane) + len(workers) - 1)

    starts = []
    for h in range(2):
        at = pl.ds(h * HALF, HALF)
        copy = pltpu.make_async_remote_copy(
            src_ref=dout_ref.at[at],
            dst_ref=dbuf.at[me, at],
            send_sem=i_send.at[h],
            recv_sem=i_recv.at[jnp.where(home, h, 2)],
            device_id={
                "dp": jnp.where(home, other, x * 2 + h),
                "seq": jnp.where(home, me, partner),
            },
            device_id_type=MESH,
        )
        copy.start()
        starts.append(copy)

    def landing(slot):
        at = pl.ds(0, HALF)
        return pltpu.make_async_remote_copy(
            src_ref=dout_ref.at[at],
            dst_ref=dbuf.at[me, at],
            send_sem=i_send.at[0],
            recv_sem=i_recv.at[slot],
            device_id=swap,
            device_id_type=MESH,
        )

    w_copy = pltpu.make_async_remote_copy(
        src_ref=w_hbm, dst_ref=w_ref, send_sem=x_send.at[0], recv_sem=x_recv.at[0],
        device_id=swap, device_id_type=MESH,
    )
    pl.when(away)(w_copy.start)

    def q_copy(dz, u, c, recv):
        z2, y2 = wrap(z, dz), 2 * core + u
        theirs = z2 * SIDE + jnp.where(core == c, y2, 3 - y2)
        return pltpu.make_async_remote_copy(
            src_ref=qkv_ref.at[:, theirs],
            dst_ref=qkvbuf.at[:, pl.ds(me * TILE, TILE)],
            send_sem=q_send.at[dz * 4 + u * 2 + c],
            recv_sem=q_recv.at[recv],
            device_id={"dp": x * 2 + c, "seq": z2 * SIDE + y2},
            device_id_type=MESH,
        )

    def q_mine(dz, u, c):
        return (2 * core + u == y) & (core == c) if dz == 0 else None

    def unless(mine, action):
        if mine is None:
            action()
        else:
            pl.when(jnp.logical_not(mine))(action)

    q_keys = [(dz, u, c) for dz in range(SIDE) for u in range(2) for c in range(2)]
    for key in q_keys:
        unless(q_mine(*key), q_copy(*key, key[0] * 4 + y).start)

    gather = Gather(dbuf, z, columns, core * HALF, d_send, d_recv)

    def launch(column):
        gather.by(column).start()
        gather.az(column, 0).start()
        gather.az(column, 1).start()
        gather.ay(0, column).start()
        gather.bz(column, 0).start()
        gather.bz(column, 1).start()

    def block_of(step):
        column = pick(step, [o[1] for o in ORDER])
        base = jnp.where(column < 2, columns[0], columns[2])
        return wrap(z, pick(step, [o[0] for o in ORDER])) * SIDE + jnp.where(
            lax.rem(column, 2) == 0, base, 3 - base
        )

    def forward(step, block):
        at = dbuf.at[block, pl.ds(pl.multiple_of(core * HALF, HALF), HALF)]
        return pltpu.make_async_remote_copy(
            src_ref=at, dst_ref=at, send_sem=f_send.at[step], recv_sem=f_recv.at[step],
            device_id={"dp": other}, device_id_type=MESH,
        )

    def pass_on(dz, column):
        forward(ORDER.index((dz, column)), gather.block(dz, column)).start()

    pl.when(home)(own_d.wait)
    pl.when(away)(landing(core).wait_recv)
    launch(0)
    landing(2).wait_recv()
    launch(1)
    pass_on(0, 1)

    tiles = mask_ref[head // (HEADS // GROUPS)]
    for j in range(BLOCKS):
        bias[:, j * TILE:(j + 1) * TILE] = jnp.broadcast_to(
            jnp.where(tiles[:, j:j + 1] > 0, 0.0, -jnp.inf), (BLOCKS, TILE)
        )
    dkt[...] = jnp.zeros_like(dkt)
    dvt[...] = jnp.zeros_like(dvt)
    gw_ref[...] = jnp.zeros_like(gw_ref)

    for column in range(2):
        gather.az(column, 0).wait_recv()
        gather.az(column, 2).start()
        gather.ay(-1, column).start()
        gather.az(column, 1).wait_recv()
        gather.az(column, 3).start()
        gather.ay(1, column).start()
    for column in range(2):
        gather.by(column).wait_recv()
        gather.bz(column + 2, 0).start()
        gather.bz(column + 2, 1).start()

    pl.when(home)(home_m.wait)
    pl.when(away)(own_m.wait)
    pl.when(away)(landing(1 - core).wait_recv)
    pl.when(home)(own_q.wait)
    pl.when(home)(own_w.wait)
    pl.when(away)(w_copy.wait_recv)
    for dz in range(SIDE):
        for source in range(SIDE):
            unless((y == source) & home if dz == 0 else None,
                   q_copy(dz, 0, 0, dz * 4 + source).wait_recv)

    mom_copy = pltpu.make_async_remote_copy(
        src_ref=mom_hbm, dst_ref=jobmom, send_sem=x_send.at[2], recv_sem=x_recv.at[2],
        device_id=swap, device_id_type=MESH,
    )
    pl.when(away)(mom_copy.start)

    def arrive(step):
        if step == 2:
            for column in range(2):
                gather.ay(0, column).wait_recv()
                pass_on(0, column + 2)
        elif step == 4:
            for column in range(2):
                gather.az(column, 2).wait_recv()
                gather.az(column, 3).wait_recv()
                gather.ay(2, column).start()
            for column in range(2):
                gather.bz(column, 0).wait_recv()
                gather.bz(column, 2).start()
                pass_on(-1, column)
                gather.bz(column, 1).wait_recv()
                gather.bz(column, 3).start()
                pass_on(1, column)
        elif step == 8:
            for column in range(2):
                gather.bz(column, 2).wait_recv()
                gather.bz(column, 3).wait_recv()
                pass_on(2, column)
            for column in range(2, 4):
                gather.bz(column, 0).wait_recv()
                gather.bz(column, 2).start()
                gather.bz(column, 1).wait_recv()
                gather.bz(column, 3).start()
        elif step == 10:
            for column in range(2):
                gather.ay(-1, column).wait_recv()
                pass_on(-1, column + 2)
        elif step == 12:
            for column in range(2):
                gather.ay(1, column).wait_recv()
                pass_on(1, column + 2)
        elif step == 14:
            for column in range(2):
                gather.bz(column + 2, 2).wait_recv()
                gather.bz(column + 2, 3).wait_recv()
                gather.ay(2, column).wait_recv()
                pass_on(2, column + 2)

    def dq_copy(step, block, recv):
        return pltpu.make_async_remote_copy(
            src_ref=dqbuf.at[pl.ds(pl.multiple_of(block * TILE, TILE), TILE)],
            dst_ref=grads_ref.at[0, head],
            send_sem=g_send.at[step],
            recv_sem=g_recv.at[recv],
            device_id={"dp": x * 2 + side, "seq": block},
            device_id_type=MESH,
        )

    def load(ref, blocks):
        return jnp.concatenate(
            [ref[pl.ds(pl.multiple_of(b * TILE, TILE), TILE), :] for b in blocks], axis=0
        )

    def body(turn, carry):
        for number in (2, 4, 8, 10, 12, 14):
            @pl.when(turn * 2 == number)
            def _():
                arrive(number)

        steps = (turn * 2, turn * 2 + 1)
        blocks = [block_of(step) for step in steps]
        pl.when(turn > 0)(forward(steps[0], blocks[0]).wait_recv)
        forward(steps[1], blocks[1]).wait_recv()
        q = load(qkvbuf.at[0], blocks)
        k = qkvbuf[1]
        v = qkvbuf[2]
        d = jnp.concatenate([dbuf[b] for b in blocks], axis=0)
        cot = nt(d, w_ref[...]).astype(jnp.bfloat16)
        hidden = jnp.concatenate(
            [jnp.broadcast_to(bias[pl.ds(b, 1), :], (TILE, bias.shape[1])) for b in blocks], axis=0
        )
        scores = nt(q, k) * inv_root + hidden
        top = jnp.max(scores, axis=-1, keepdims=True)
        expo = jnp.exp(scores - top)
        probs = expo * (1.0 / jnp.sum(expo, axis=-1, keepdims=True))
        probs_b = probs.astype(jnp.bfloat16)
        att = nn(probs_b, v).astype(jnp.bfloat16)
        delta = jnp.sum(
            cot.astype(jnp.float32) * att.astype(jnp.float32), axis=-1, keepdims=True
        )
        dscores = (probs * (nt(cot, v) - delta)).astype(jnp.bfloat16)
        dq = (nn(dscores, k) * inv_root).astype(jnp.bfloat16)
        for index, block in enumerate(blocks):
            dqbuf[pl.ds(pl.multiple_of(block * TILE, TILE), TILE), :] = (
                dq[index * TILE:(index + 1) * TILE]
            )
        for step, block in zip(steps, blocks):
            hop = lax.rem(pick(step, [o[0] for o in ORDER]) + SIDE, SIDE)
            pl.when((step > 0) | away)(dq_copy(step, block, hop * 4 + slot_of_job).start)

        dkt[...] += tn(q, dscores)
        dvt[...] += tn(cot, probs_b)
        gw_ref[...] += tn(att, d)
        return carry

    lax.fori_loop(0, BLOCKS // 2, body, 0)

    gw_copy = pltpu.make_async_remote_copy(
        src_ref=gwout, dst_ref=gwin, send_sem=x_send.at[1], recv_sem=x_recv.at[1],
        device_id=swap, device_id_type=MESH,
    )

    def rows_at(index):
        return pl.ds(pl.multiple_of(index * rows, rows), rows)

    def compress_all(mom, grad, sent):
        def moment(index, total):
            at = rows_at(index)
            value = 0.9 * mom[at, :] + 0.1 * grad[at, :].astype(jnp.float32)
            mom[at, :] = value
            return total + jnp.abs(value)

        total = lax.fori_loop(0, WORKERS, moment, jnp.zeros((rows, width), jnp.float32))
        scale = jnp.sum(total, axis=(0, 1), keepdims=True) / (rows * WORKERS * width) + 1e-06
        unscale = 1.0 / scale

        def compress(index, carry):
            at = rows_at(index)
            value = mom[at, :]
            code = (scale * jnp.tanh(value * unscale)).astype(jnp.bfloat16)
            if sent is not None:
                sent[at, :] = code
            werrbuf[at, :] = value - code.astype(jnp.float32)
            return carry

        lax.fori_loop(0, WORKERS, compress, 0)

    gwout[...] = gw_ref[...].astype(jnp.bfloat16)

    @pl.when(away)
    def _():
        mom_copy.wait_recv()

    compress_all(jobmom, gwout, sentbuf)

    turns = (2, 1, 3)

    def pair(index):
        return pl.ds(pl.multiple_of(index * 2 * rows, 2 * rows), 2 * rows)

    m_copies = []
    for index, dx in enumerate(turns):
        copy = pltpu.make_async_remote_copy(
            src_ref=sentbuf.at[pair(wrap(x, dx))],
            dst_ref=landed.at[x],
            send_sem=m_send.at[index],
            recv_sem=m_recv.at[index],
            device_id={"dp": wrap(x, dx) * 2 + core},
            device_id_type=MESH,
        )
        copy.start()
        m_copies.append(copy)
    landed[x] = sentbuf[pair(x), :]
    werr_out = pltpu.make_async_copy(werrbuf, werr_ref, local_sem.at[4])
    pl.when(home)(werr_out.start)

    kvbuf[0] = (dkt[...].T * inv_root).astype(jnp.bfloat16)
    kvbuf[1] = dvt[...].T.astype(jnp.bfloat16)

    def kv_copy(dz, target, recv):
        block = wrap(z, dz) * SIDE + target
        return pltpu.make_async_remote_copy(
            src_ref=kvbuf.at[:, pl.ds(pl.multiple_of(block * TILE, TILE), TILE)],
            dst_ref=grads_ref.at[pl.ds(1, 2), head],
            send_sem=kv_send.at[dz * 4 + target],
            recv_sem=kv_recv.at[recv],
            device_id={"dp": x * 2 + side, "seq": block},
            device_id_type=MESH,
        )

    def kv_mine(dz, target):
        return (y == target) & home if dz == 0 else None

    kv_keys = [(dz, target) for dz in (2, 1, 3, 0) for target in range(SIDE)]
    for key in kv_keys:
        unless(kv_mine(*key), kv_copy(*key, key[0] * 4 + slot_of_job).start)
    own_kv = pltpu.make_async_copy(
        kvbuf.at[:, pl.ds(pl.multiple_of(me * TILE, TILE), TILE)],
        grads_ref.at[pl.ds(1, 2), me],
        local_sem.at[5],
    )
    own_dq = pltpu.make_async_copy(
        dqbuf.at[pl.ds(pl.multiple_of(me * TILE, TILE), TILE)], grads_ref.at[0, me], local_sem.at[6]
    )

    @pl.when(home)
    def _():
        own_kv.start()
        own_dq.start()

    for copy in m_copies:
        copy.wait_recv()
    partial = landed[0].astype(jnp.float32)
    for index in range(1, SIDE):
        partial = partial + landed[index].astype(jnp.float32)
    partial = partial.astype(jnp.bfloat16)
    parts[0] = partial[:rows]
    parts[1] = partial[rows:]

    def part_copy(c, recv, seq):
        return pltpu.make_async_remote_copy(
            src_ref=parts.at[c],
            dst_ref=sums.at[recv],
            send_sem=p_send.at[c],
            recv_sem=p_recv.at[recv],
            device_id={"dp": x * 2 + c, "seq": seq},
            device_id_type=MESH,
        )

    @pl.when(home)
    def _():
        part_copy(1 - core, 0, me).start()
        sums[0] = parts[core]

    @pl.when(away)
    def _():
        part_copy(0, 1, partner).start()
        part_copy(1, 1, partner).start()
        gw_copy.start()
        part_copy(0, 0, me).wait_recv()

    part_copy(0, 1, partner).wait_recv()

    average = (sums[0].astype(jnp.float32) + sums[1].astype(jnp.float32)) / WORKERS
    server = jnp.sum(jnp.abs(average), axis=(0, 1), keepdims=True) / (rows * width) + 1e-06
    code = (server * jnp.tanh(average * (1.0 / server))).astype(jnp.bfloat16)
    syncbuf[rows_at(worker), :] = code
    serrbuf[...] = average - code.astype(jnp.float32)

    def sync_copy(slot, index, dp):
        at = syncbuf.at[rows_at(index)]
        return pltpu.make_async_remote_copy(
            src_ref=at, dst_ref=at, send_sem=s_send.at[slot], recv_sem=s_recv.at[slot],
            device_id={"dp": dp}, device_id_type=MESH,
        )

    for slot, dx in enumerate(turns):
        sync_copy(slot, worker, wrap(x, dx) * 2 + core).start()
    sync_copy(3, worker, other).start()
    serr_out = pltpu.make_async_copy(serrbuf, serr_ref, local_sem.at[8])
    serr_out.start()

    @pl.when(away)
    def _():
        gw_copy.wait_recv()
        compress_all(mom_ref, gwin, None)
        werr_out.start()

    for slot, dx in enumerate(turns):
        sync_copy(slot, worker, other).wait_recv()
        sync_copy(4 + slot, wrap(x, -dx) * 2 + core, other).start()
    for slot in range(3, 7):
        sync_copy(slot, worker, other).wait_recv()
    own_s = pltpu.make_async_copy(syncbuf, sync_ref, local_sem.at[7])
    own_s.start()

    for key in q_keys:
        unless(q_mine(*key), q_copy(*key, 0).wait_send)
    for copy in gather.every() + starts + m_copies:
        copy.wait_send()
    for slot in range(7):
        sync_copy(slot, worker, other).wait_send()

    @pl.when(home)
    def _():
        part_copy(1 - core, 0, me).wait_send()

    @pl.when(away)
    def _():
        part_copy(0, 1, partner).wait_send()
        part_copy(1, 1, partner).wait_send()
        w_copy.wait_send()
        mom_copy.wait_send()
        gw_copy.wait_send()

    for step in range(1, BLOCKS):
        forward(step, me).wait_send()

    for step in range(BLOCKS):
        unless(home if step == 0 else None, dq_copy(step, me, 0).wait_send)
    for key in kv_keys:
        unless(kv_mine(*key), kv_copy(*key, 0).wait_send)
    for slot in range(BLOCKS):
        mine = home & (slot_of_job == slot) if slot < 4 else None
        unless(mine, dq_copy(0, me, slot).wait_recv)
        unless(mine, kv_copy(0, 0, slot).wait_recv)

    @pl.when(home)
    def _():
        own_kv.wait()
        own_dq.wait()

    for copy in (own_s, werr_out, serr_out):
        copy.wait()


def body(qkv, tile_mask, d_out, w_out, momentum):
    tokens, head_size = qkv.shape[2], qkv.shape[4]
    width = d_out.shape[2]
    length = tokens * BLOCKS
    inv_root = 1.0 / math.sqrt(head_size)
    rows = head_size // WORKERS
    qkv_t = jnp.transpose(qkv[:, 0], (0, 2, 1, 3))
    vmem = pl.BlockSpec(memory_space=pltpu.VMEM)
    hbm = pl.BlockSpec(memory_space=pl.ANY)
    dma = pltpu.SemaphoreType.DMA
    grads, synced, worker_error, server_error = pl.pallas_call(
        functools.partial(kernel, inv_root),
        out_shape=(
            jax.ShapeDtypeStruct((3, HEADS, tokens, head_size), jnp.bfloat16),
            jax.ShapeDtypeStruct((head_size, width), jnp.bfloat16),
            jax.ShapeDtypeStruct((head_size, width), jnp.float32),
            jax.ShapeDtypeStruct((rows, width), jnp.float32),
        ),
        in_specs=[hbm, hbm, hbm, vmem, hbm],
        out_specs=(hbm, hbm, hbm, hbm),
        scratch_shapes=[
            pltpu.VMEM((3, length, head_size), jnp.bfloat16),
            pltpu.VMEM((BLOCKS, tokens, width), jnp.bfloat16),
            pltpu.VMEM((head_size, width), jnp.bfloat16),
            pltpu.VMEM((head_size, width), jnp.float32),
            pltpu.VMEM((BLOCKS, length), jnp.float32),
            pltpu.VMEM((length, head_size), jnp.bfloat16),
            pltpu.VMEM((head_size, length), jnp.float32),
            pltpu.VMEM((head_size, length), jnp.float32),
            pltpu.VMEM((2, length, head_size), jnp.bfloat16),
            pltpu.VMEM((head_size, width), jnp.float32),
            pltpu.VMEM((head_size, width), jnp.bfloat16),
            pltpu.VMEM((head_size, width), jnp.float32),
            pltpu.VMEM((SIDE, 2 * rows, width), jnp.bfloat16),
            pltpu.VMEM((2, rows, width), jnp.bfloat16),
            pltpu.VMEM((2, rows, width), jnp.bfloat16),
            pltpu.VMEM((head_size, width), jnp.bfloat16),
            pltpu.VMEM((rows, width), jnp.float32),
            pltpu.VMEM((head_size, width), jnp.bfloat16),
            pltpu.VMEM((head_size, width), jnp.bfloat16),
            pltpu.VMEM((head_size, width), jnp.float32),
            dma((BLOCKS,)), dma((BLOCKS,)),
            dma((34,)), dma((34,)),
            dma((BLOCKS,)), dma((BLOCKS,)),
            dma((2,)), dma((3,)),
            dma((BLOCKS,)), dma((BLOCKS,)),
            dma((BLOCKS,)), dma((BLOCKS,)),
            dma((3,)), dma((3,)),
            dma((SIDE - 1,)), dma((SIDE - 1,)),
            dma((2,)), dma((2,)),
            dma((WORKERS - 1,)), dma((WORKERS - 1,)),
            dma((9,)),
        ],
        compiler_params=pltpu.CompilerParams(
            collective_id=0, has_side_effects=True, vmem_limit_bytes=56 << 20
        ),
    )(qkv_t, d_out[0], w_out[0], tile_mask, momentum[0])
    grad_qkv = jnp.transpose(grads, (0, 2, 1, 3))[:, None]
    return (grad_qkv, synced[None], worker_error[None, None], server_error[None])


def solution(mesh):
    placed = (
        P(None, "dp", "seq", None, None),
        P(),
        P("dp", "seq", None),
        P("seq", None, None),
        P("seq", None, None),
    )
    return jax.shard_map(
        body,
        mesh=mesh,
        in_specs=placed,
        out_specs=(
            P(None, "dp", "seq", None, None),
            P("seq", None, None),
            P("dp", "seq", None, None),
            P("seq", "dp", None),
        ),
        check_vma=False,
    )
```

```python
import functools
import math

import jax
import jax.numpy as jnp
from jax import lax
from jax.experimental import pallas as pl
from jax.experimental.pallas import tpu as pltpu
from jax.sharding import PartitionSpec as P

HEADS = 16
GROUPS = 8
TILE = 128
SIDE = 4
BLOCKS = SIDE * SIDE
WORKERS = 8
HALF = TILE // 2
PART = HALF // 2
MESH = pl.DeviceIdType.MESH

ORDER = (
    (0, 0), (0, 1), (0, 2), (0, 3),
    (-1, 0), (-1, 1), (1, 0), (1, 1),
    (2, 0), (2, 1),
    (-1, 2), (-1, 3), (1, 2), (1, 3),
    (2, 2), (2, 3),
)
OFFSETS = (0, -1, 1, 2)


def wrap(position, offset):
    return lax.rem(position + (offset + SIDE), SIDE)


def pick(step, table):
    value = jnp.int32(table[0])
    for index, entry in enumerate(table):
        if index and entry != table[0]:
            value = jnp.where(step == index, jnp.int32(entry), value)
    return value


def nt(a, b):
    return lax.dot_general(a, b, (((1,), (1,)), ((), ())), preferred_element_type=jnp.float32)


def nn(a, b):
    return lax.dot_general(a, b, (((1,), (0,)), ((), ())), preferred_element_type=jnp.float32)


def tn(a, b):
    return lax.dot_general(a, b, (((0,), (0,)), ((), ())), preferred_element_type=jnp.float32)


class Gather:
    def __init__(self, buf, z, columns, row0, send, recv):
        self.buf, self.z, self.columns, self.row0 = buf, z, columns, row0
        self.send, self.recv = send, recv

    def block(self, dz, column):
        return wrap(self.z, dz) * SIDE + self.columns[column]

    def copy(self, slot, block, lo, n, dz, column):
        rows = self.buf.at[block, pl.ds(pl.multiple_of(self.row0 + lo, PART // 2), n)]
        return pltpu.make_async_remote_copy(
            src_ref=rows,
            dst_ref=rows,
            send_sem=self.send.at[slot],
            recv_sem=self.recv.at[slot],
            device_id={"seq": self.block(dz, column)},
            device_id_type=MESH,
        )

    def ring(self, slot, column, kind, lo):
        if kind == 0:
            return self.copy(slot, self.block(0, column), lo, PART, 1, 0)
        if kind == 1:
            return self.copy(slot, self.block(0, column), lo, PART, -1, 0)
        if kind == 2:
            return self.copy(slot, self.block(-1, column), lo, PART // 2, 1, 0)
        return self.copy(slot, self.block(1, column), lo + PART // 2, PART // 2, -1, 0)

    def az(self, column, kind):
        return self.ring(column * 4 + kind, column, kind, 0)

    def ay(self, dz, column):
        slot = 8 + OFFSETS.index(dz) * 2 + column
        return self.copy(slot, self.block(dz, column), 0, PART, 0, 2)

    def by(self, column):
        return self.copy(16 + column, self.block(0, column), PART, PART, 0, 2)

    def bz(self, column, kind):
        return self.ring(18 + column * 4 + kind, column, kind, PART)

    def every(self):
        copies = [self.az(c, kind) for c in range(2) for kind in range(4)]
        copies += [self.ay(dz, c) for dz in OFFSETS for c in range(2)]
        copies += [self.by(c) for c in range(2)]
        return copies + [self.bz(c, kind) for c in range(4) for kind in range(4)]


def kernel(
    inv_root,
    qkv_ref, dout_ref, w_hbm, mask_ref, mom_hbm,
    grads_ref, sync_ref, werr_ref, serr_ref,
    tokenwise, headwise, qkvbuf, dbuf, w_ref, mom_ref, bias, dqbuf, dkt, dvt, kvbuf, gw_ref,
    sentbuf, werrbuf, landed, parts, sums, syncbuf, serrbuf, gwout, gwin, jobmom,
    q_in, q_send, q_recv, d_send, d_recv, f_send, f_recv, i_send, i_recv,
    g_send, g_recv, kv_send, kv_recv, x_send, x_recv,
    m_send, m_recv, p_send, p_recv, s_send, s_recv, local_sem,
):
    me = lax.axis_index("seq")
    z = me // SIDE
    y = lax.rem(me, SIDE)
    worker = lax.axis_index("dp")
    x = worker // 2
    core = lax.rem(worker, 2)
    width = dout_ref.shape[1]
    rows = sentbuf.shape[0] // WORKERS

    side = y // 2
    home = core == side
    away = core != side
    columns = (y, 3 - y, y + 1 - 2 * lax.rem(y, 2), 2 - y + 2 * lax.rem(y, 2))
    other = x * 2 + 1 - core
    partner = z * SIDE + 3 - y
    head = jnp.where(home, me, partner)
    swap = {"dp": other, "seq": partner}
    slot_of_job = lax.rem(y, 2) * 2 + core

    own_d = pltpu.make_async_copy(dout_ref, dbuf.at[me], local_sem.at[0])
    all_q = [pltpu.make_async_copy(qkv_ref.at[p], tokenwise.at[p], q_in.at[p]) for p in range(3)]
    for copy in all_q:
        copy.start()
    own_q = pltpu.make_async_copy(
        headwise.at[:, me], qkvbuf.at[:, pl.ds(me * TILE, TILE)], local_sem.at[1]
    )
    own_w = pltpu.make_async_copy(w_hbm, w_ref, local_sem.at[2])
    own_m = pltpu.make_async_copy(mom_hbm, mom_ref, local_sem.at[3])
    home_m = pltpu.make_async_copy(mom_hbm, jobmom, local_sem.at[3])

    @pl.when(home)
    def _():
        own_d.start()
        own_w.start()
        home_m.start()

    pl.when(away)(own_m.start)

    workers = [
        wrap(x, dx) * 2 + lax.rem(core + dc, 2)
        for dx in (2, 1, -1, 0) for dc in range(2) if (dx, dc) != (0, 0)
    ]
    plane = [
        (x * 2 + lax.rem(core + dc, 2), wrap(z, dz) * SIDE + wrap(y, dy))
        for dc in range(2) for dz in range(SIDE) for dy in range(SIDE) if (dc, dz, dy) != (0, 0, 0)
    ]
    barrier = pltpu.get_barrier_semaphore()
    for dp, seq in plane:
        pl.semaphore_signal(
            barrier, inc=1, device_id={"dp": dp, "seq": seq}, device_id_type=MESH
        )
    for peer in workers[:-1]:
        pl.semaphore_signal(barrier, inc=1, device_id={"dp": peer}, device_id_type=MESH)
    pl.semaphore_wait(barrier, len(plane) + len(workers) - 1)

    starts = []
    for h in range(2):
        at = pl.ds(h * HALF, HALF)
        copy = pltpu.make_async_remote_copy(
            src_ref=dout_ref.at[at],
            dst_ref=dbuf.at[me, at],
            send_sem=i_send.at[h],
            recv_sem=i_recv.at[jnp.where(home, h, 2)],
            device_id={
                "dp": jnp.where(home, other, x * 2 + h),
                "seq": jnp.where(home, me, partner),
            },
            device_id_type=MESH,
        )
        copy.start()
        starts.append(copy)

    def landing(slot):
        at = pl.ds(0, HALF)
        return pltpu.make_async_remote_copy(
            src_ref=dout_ref.at[at],
            dst_ref=dbuf.at[me, at],
            send_sem=i_send.at[0],
            recv_sem=i_recv.at[slot],
            device_id=swap,
            device_id_type=MESH,
        )

    w_copy = pltpu.make_async_remote_copy(
        src_ref=w_hbm, dst_ref=w_ref, send_sem=x_send.at[0], recv_sem=x_recv.at[0],
        device_id=swap, device_id_type=MESH,
    )
    pl.when(away)(w_copy.start)

    def q_copy(dz, u, c, recv):
        z2, y2 = wrap(z, dz), 2 * core + u
        theirs = z2 * SIDE + jnp.where(core == c, y2, 3 - y2)
        return pltpu.make_async_remote_copy(
            src_ref=headwise.at[:, theirs],
            dst_ref=qkvbuf.at[:, pl.ds(me * TILE, TILE)],
            send_sem=q_send.at[dz * 4 + u * 2 + c],
            recv_sem=q_recv.at[recv],
            device_id={"dp": x * 2 + c, "seq": z2 * SIDE + y2},
            device_id_type=MESH,
        )

    def q_mine(dz, u, c):
        return (2 * core + u == y) & (core == c) if dz == 0 else None

    def unless(mine, action):
        if mine is None:
            action()
        else:
            pl.when(jnp.logical_not(mine))(action)

    q_keys = [(dz, u, c) for dz in range(SIDE) for u in range(2) for c in range(2)]
    for p in range(3):
        all_q[p].wait()
        headwise[p] = jnp.swapaxes(tokenwise[p], 0, 1)
    for key in q_keys:
        unless(q_mine(*key), q_copy(*key, key[0] * 4 + y).start)
    pl.when(home)(own_q.start)

    gather = Gather(dbuf, z, columns, core * HALF, d_send, d_recv)

    def launch(column):
        gather.by(column).start()
        gather.az(column, 0).start()
        gather.az(column, 1).start()
        gather.ay(0, column).start()
        gather.bz(column, 0).start()
        gather.bz(column, 1).start()

    def block_of(step):
        column = pick(step, [o[1] for o in ORDER])
        base = jnp.where(column < 2, columns[0], columns[2])
        return wrap(z, pick(step, [o[0] for o in ORDER])) * SIDE + jnp.where(
            lax.rem(column, 2) == 0, base, 3 - base
        )

    def forward(step, block):
        at = dbuf.at[block, pl.ds(pl.multiple_of(core * HALF, HALF), HALF)]
        return pltpu.make_async_remote_copy(
            src_ref=at, dst_ref=at, send_sem=f_send.at[step], recv_sem=f_recv.at[step],
            device_id={"dp": other}, device_id_type=MESH,
        )

    def pass_on(dz, column):
        forward(ORDER.index((dz, column)), gather.block(dz, column)).start()

    pl.when(home)(own_d.wait)
    pl.when(away)(landing(core).wait_recv)
    launch(0)
    landing(2).wait_recv()
    launch(1)
    pass_on(0, 1)

    tiles = mask_ref[head // (HEADS // GROUPS)]
    for j in range(BLOCKS):
        bias[:, j * TILE:(j + 1) * TILE] = jnp.broadcast_to(
            jnp.where(tiles[:, j:j + 1] > 0, 0.0, -jnp.inf), (BLOCKS, TILE)
        )
    dkt[...] = jnp.zeros_like(dkt)
    dvt[...] = jnp.zeros_like(dvt)
    gw_ref[...] = jnp.zeros_like(gw_ref)

    for column in range(2):
        gather.az(column, 0).wait_recv()
        gather.az(column, 2).start()
        gather.ay(-1, column).start()
        gather.az(column, 1).wait_recv()
        gather.az(column, 3).start()
        gather.ay(1, column).start()
    for column in range(2):
        gather.by(column).wait_recv()
        gather.bz(column + 2, 0).start()
        gather.bz(column + 2, 1).start()

    pl.when(home)(home_m.wait)
    pl.when(away)(own_m.wait)
    pl.when(away)(landing(1 - core).wait_recv)
    pl.when(home)(own_q.wait)
    pl.when(home)(own_w.wait)
    pl.when(away)(w_copy.wait_recv)
    for dz in range(SIDE):
        for source in range(SIDE):
            unless((y == source) & home if dz == 0 else None,
                   q_copy(dz, 0, 0, dz * 4 + source).wait_recv)

    mom_copy = pltpu.make_async_remote_copy(
        src_ref=mom_hbm, dst_ref=jobmom, send_sem=x_send.at[2], recv_sem=x_recv.at[2],
        device_id=swap, device_id_type=MESH,
    )
    pl.when(away)(mom_copy.start)

    def arrive(step):
        if step == 2:
            for column in range(2):
                gather.ay(0, column).wait_recv()
                pass_on(0, column + 2)
        elif step == 4:
            for column in range(2):
                gather.az(column, 2).wait_recv()
                gather.az(column, 3).wait_recv()
                gather.ay(2, column).start()
            for column in range(2):
                gather.bz(column, 0).wait_recv()
                gather.bz(column, 2).start()
                pass_on(-1, column)
                gather.bz(column, 1).wait_recv()
                gather.bz(column, 3).start()
                pass_on(1, column)
        elif step == 8:
            for column in range(2):
                gather.bz(column, 2).wait_recv()
                gather.bz(column, 3).wait_recv()
                pass_on(2, column)
            for column in range(2, 4):
                gather.bz(column, 0).wait_recv()
                gather.bz(column, 2).start()
                gather.bz(column, 1).wait_recv()
                gather.bz(column, 3).start()
        elif step == 10:
            for column in range(2):
                gather.ay(-1, column).wait_recv()
                pass_on(-1, column + 2)
        elif step == 12:
            for column in range(2):
                gather.ay(1, column).wait_recv()
                pass_on(1, column + 2)
        elif step == 14:
            for column in range(2):
                gather.bz(column + 2, 2).wait_recv()
                gather.bz(column + 2, 3).wait_recv()
                gather.ay(2, column).wait_recv()
                pass_on(2, column + 2)

    def dq_copy(step, block, recv):
        return pltpu.make_async_remote_copy(
            src_ref=dqbuf.at[pl.ds(pl.multiple_of(block * TILE, TILE), TILE)],
            dst_ref=grads_ref.at[0, head],
            send_sem=g_send.at[step],
            recv_sem=g_recv.at[recv],
            device_id={"dp": x * 2 + side, "seq": block},
            device_id_type=MESH,
        )

    def load(ref, blocks):
        return jnp.concatenate(
            [ref[pl.ds(pl.multiple_of(b * TILE, TILE), TILE), :] for b in blocks], axis=0
        )

    def body(turn, carry):
        for number in (2, 4, 8, 10, 12, 14):
            @pl.when(turn * 2 == number)
            def _():
                arrive(number)

        steps = (turn * 2, turn * 2 + 1)
        blocks = [block_of(step) for step in steps]
        pl.when(turn > 0)(forward(steps[0], blocks[0]).wait_recv)
        forward(steps[1], blocks[1]).wait_recv()
        q = load(qkvbuf.at[0], blocks)
        k = qkvbuf[1]
        v = qkvbuf[2]
        d = jnp.concatenate([dbuf[b] for b in blocks], axis=0)
        cot = nt(d, w_ref[...]).astype(jnp.bfloat16)
        hidden = jnp.concatenate(
            [jnp.broadcast_to(bias[pl.ds(b, 1), :], (TILE, bias.shape[1])) for b in blocks], axis=0
        )
        scores = nt(q, k) * inv_root + hidden
        top = jnp.max(scores, axis=-1, keepdims=True)
        expo = jnp.exp(scores - top)
        probs = expo * (1.0 / jnp.sum(expo, axis=-1, keepdims=True))
        probs_b = probs.astype(jnp.bfloat16)
        att = nn(probs_b, v).astype(jnp.bfloat16)
        delta = jnp.sum(
            cot.astype(jnp.float32) * att.astype(jnp.float32), axis=-1, keepdims=True
        )
        dscores = (probs * (nt(cot, v) - delta)).astype(jnp.bfloat16)
        dq = (nn(dscores, k) * inv_root).astype(jnp.bfloat16)
        for index, block in enumerate(blocks):
            dqbuf[pl.ds(pl.multiple_of(block * TILE, TILE), TILE), :] = (
                dq[index * TILE:(index + 1) * TILE]
            )
        for step, block in zip(steps, blocks):
            hop = lax.rem(pick(step, [o[0] for o in ORDER]) + SIDE, SIDE)
            pl.when((step > 0) | away)(dq_copy(step, block, hop * 4 + slot_of_job).start)

        dkt[...] += tn(q, dscores)
        dvt[...] += tn(cot, probs_b)
        gw_ref[...] += tn(att, d)
        return carry

    lax.fori_loop(0, BLOCKS // 2, body, 0)

    gw_copy = pltpu.make_async_remote_copy(
        src_ref=gwout, dst_ref=gwin, send_sem=x_send.at[1], recv_sem=x_recv.at[1],
        device_id=swap, device_id_type=MESH,
    )

    def rows_at(index):
        return pl.ds(pl.multiple_of(index * rows, rows), rows)

    def compress_all(mom, grad, sent):
        def moment(index, total):
            at = rows_at(index)
            value = 0.9 * mom[at, :] + 0.1 * grad[at, :].astype(jnp.float32)
            mom[at, :] = value
            return total + jnp.abs(value)

        total = lax.fori_loop(0, WORKERS, moment, jnp.zeros((rows, width), jnp.float32))
        scale = jnp.sum(total, axis=(0, 1), keepdims=True) / (rows * WORKERS * width) + 1e-06
        unscale = 1.0 / scale

        def compress(index, carry):
            at = rows_at(index)
            value = mom[at, :]
            code = (scale * jnp.tanh(value * unscale)).astype(jnp.bfloat16)
            if sent is not None:
                sent[at, :] = code
            werrbuf[at, :] = value - code.astype(jnp.float32)
            return carry

        lax.fori_loop(0, WORKERS, compress, 0)

    kvbuf[0] = (dkt[...].T * inv_root).astype(jnp.bfloat16)
    kvbuf[1] = dvt[...].T.astype(jnp.bfloat16)

    def kv_copy(dz, target, recv):
        block = wrap(z, dz) * SIDE + target
        return pltpu.make_async_remote_copy(
            src_ref=kvbuf.at[:, pl.ds(pl.multiple_of(block * TILE, TILE), TILE)],
            dst_ref=grads_ref.at[pl.ds(1, 2), head],
            send_sem=kv_send.at[dz * 4 + target],
            recv_sem=kv_recv.at[recv],
            device_id={"dp": x * 2 + side, "seq": block},
            device_id_type=MESH,
        )

    def kv_mine(dz, target):
        return (y == target) & home if dz == 0 else None

    kv_keys = [(dz, target) for dz in (2, 1, 3, 0) for target in range(SIDE)]
    for key in kv_keys:
        unless(kv_mine(*key), kv_copy(*key, key[0] * 4 + slot_of_job).start)
    own_kv = pltpu.make_async_copy(
        kvbuf.at[:, pl.ds(pl.multiple_of(me * TILE, TILE), TILE)],
        grads_ref.at[pl.ds(1, 2), me],
        local_sem.at[5],
    )
    own_dq = pltpu.make_async_copy(
        dqbuf.at[pl.ds(pl.multiple_of(me * TILE, TILE), TILE)], grads_ref.at[0, me], local_sem.at[6]
    )

    @pl.when(home)
    def _():
        own_kv.start()
        own_dq.start()

    gwout[...] = gw_ref[...].astype(jnp.bfloat16)

    @pl.when(away)
    def _():
        mom_copy.wait_recv()

    compress_all(jobmom, gwout, sentbuf)

    turns = (2, 1, 3)

    def pair(index):
        return pl.ds(pl.multiple_of(index * 2 * rows, 2 * rows), 2 * rows)

    m_copies = []
    for index, dx in enumerate(turns):
        copy = pltpu.make_async_remote_copy(
            src_ref=sentbuf.at[pair(wrap(x, dx))],
            dst_ref=landed.at[x],
            send_sem=m_send.at[index],
            recv_sem=m_recv.at[index],
            device_id={"dp": wrap(x, dx) * 2 + core},
            device_id_type=MESH,
        )
        copy.start()
        m_copies.append(copy)
    landed[x] = sentbuf[pair(x), :]
    werr_out = pltpu.make_async_copy(werrbuf, werr_ref, local_sem.at[4])
    pl.when(home)(werr_out.start)

    for copy in m_copies:
        copy.wait_recv()
    partial = landed[0].astype(jnp.float32)
    for index in range(1, SIDE):
        partial = partial + landed[index].astype(jnp.float32)
    partial = partial.astype(jnp.bfloat16)
    parts[0] = partial[:rows]
    parts[1] = partial[rows:]

    def part_copy(c, recv, seq):
        return pltpu.make_async_remote_copy(
            src_ref=parts.at[c],
            dst_ref=sums.at[recv],
            send_sem=p_send.at[c],
            recv_sem=p_recv.at[recv],
            device_id={"dp": x * 2 + c, "seq": seq},
            device_id_type=MESH,
        )

    @pl.when(home)
    def _():
        part_copy(1 - core, 0, me).start()
        sums[0] = parts[core]

    @pl.when(away)
    def _():
        part_copy(0, 1, partner).start()
        part_copy(1, 1, partner).start()
        gw_copy.start()
        part_copy(0, 0, me).wait_recv()

    part_copy(0, 1, partner).wait_recv()

    average = (sums[0].astype(jnp.float32) + sums[1].astype(jnp.float32)) / WORKERS
    server = jnp.sum(jnp.abs(average), axis=(0, 1), keepdims=True) / (rows * width) + 1e-06
    code = (server * jnp.tanh(average * (1.0 / server))).astype(jnp.bfloat16)
    syncbuf[rows_at(worker), :] = code
    serrbuf[...] = average - code.astype(jnp.float32)

    def sync_copy(slot, index, dp):
        at = syncbuf.at[rows_at(index)]
        return pltpu.make_async_remote_copy(
            src_ref=at, dst_ref=at, send_sem=s_send.at[slot], recv_sem=s_recv.at[slot],
            device_id={"dp": dp}, device_id_type=MESH,
        )

    for slot, dx in enumerate(turns):
        sync_copy(slot, worker, wrap(x, dx) * 2 + core).start()
    sync_copy(3, worker, other).start()
    serr_out = pltpu.make_async_copy(serrbuf, serr_ref, local_sem.at[8])
    serr_out.start()

    @pl.when(away)
    def _():
        gw_copy.wait_recv()
        compress_all(mom_ref, gwin, None)
        werr_out.start()

    for slot, dx in enumerate(turns):
        sync_copy(slot, worker, other).wait_recv()
        sync_copy(4 + slot, wrap(x, -dx) * 2 + core, other).start()
    for slot in range(3, 7):
        sync_copy(slot, worker, other).wait_recv()
    own_s = pltpu.make_async_copy(syncbuf, sync_ref, local_sem.at[7])
    own_s.start()

    for key in q_keys:
        unless(q_mine(*key), q_copy(*key, 0).wait_send)
    for copy in gather.every() + starts + m_copies:
        copy.wait_send()
    for slot in range(7):
        sync_copy(slot, worker, other).wait_send()

    @pl.when(home)
    def _():
        part_copy(1 - core, 0, me).wait_send()

    @pl.when(away)
    def _():
        part_copy(0, 1, partner).wait_send()
        part_copy(1, 1, partner).wait_send()
        w_copy.wait_send()
        mom_copy.wait_send()
        gw_copy.wait_send()

    for step in range(1, BLOCKS):
        forward(step, me).wait_send()

    for step in range(BLOCKS):
        unless(home if step == 0 else None, dq_copy(step, me, 0).wait_send)
    for key in kv_keys:
        unless(kv_mine(*key), kv_copy(*key, 0).wait_send)
    for slot in range(BLOCKS):
        mine = home & (slot_of_job == slot) if slot < 4 else None
        unless(mine, dq_copy(0, me, slot).wait_recv)
        unless(mine, kv_copy(0, 0, slot).wait_recv)

    @pl.when(home)
    def _():
        own_kv.wait()
        own_dq.wait()

    for copy in (own_s, werr_out, serr_out):
        copy.wait()


def finish(
    grads_in, sync_in, werr_in, serr_in, grads_out, sync_out, werr_out, serr_out,
    before, after, sync, werr, serr, in_sem, out_sem,
):
    loads = [pltpu.make_async_copy(grads_in.at[p], before.at[p], in_sem.at[p]) for p in range(3)]
    stores = [pltpu.make_async_copy(after.at[p], grads_out.at[p], out_sem.at[p]) for p in range(3)]
    plain = ((werr_in, werr, werr_out), (sync_in, sync, sync_out), (serr_in, serr, serr_out))
    for index, (source, buf, target) in enumerate(plain):
        loads.append(pltpu.make_async_copy(source, buf, in_sem.at[3 + index]))
        stores.append(pltpu.make_async_copy(buf, target, out_sem.at[3 + index]))
    for load in loads:
        load.start()
    for p in range(3):
        loads[p].wait()
        after[p] = jnp.swapaxes(before[p], 0, 1)
        stores[p].start()
        loads[3 + p].wait()
        stores[3 + p].start()
    for store in stores:
        store.wait()


def body(qkv, tile_mask, d_out, w_out, momentum):
    tokens, head_size = qkv.shape[2], qkv.shape[4]
    width = d_out.shape[2]
    length = tokens * BLOCKS
    inv_root = 1.0 / math.sqrt(head_size)
    rows = head_size // WORKERS
    vmem = pl.BlockSpec(memory_space=pltpu.VMEM)
    hbm = pl.BlockSpec(memory_space=pl.ANY)
    dma = pltpu.SemaphoreType.DMA
    grads, synced, worker_error, server_error = pl.pallas_call(
        functools.partial(kernel, inv_root),
        out_shape=(
            jax.ShapeDtypeStruct((3, HEADS, tokens, head_size), jnp.bfloat16),
            jax.ShapeDtypeStruct((head_size, width), jnp.bfloat16),
            jax.ShapeDtypeStruct((head_size, width), jnp.float32),
            jax.ShapeDtypeStruct((rows, width), jnp.float32),
        ),
        in_specs=[hbm, hbm, hbm, vmem, hbm],
        out_specs=(hbm, hbm, hbm, hbm),
        scratch_shapes=[
            pltpu.VMEM((3, tokens, HEADS, head_size), jnp.bfloat16),
            pltpu.VMEM((3, HEADS, tokens, head_size), jnp.bfloat16),
            pltpu.VMEM((3, length, head_size), jnp.bfloat16),
            pltpu.VMEM((BLOCKS, tokens, width), jnp.bfloat16),
            pltpu.VMEM((head_size, width), jnp.bfloat16),
            pltpu.VMEM((head_size, width), jnp.float32),
            pltpu.VMEM((BLOCKS, length), jnp.float32),
            pltpu.VMEM((length, head_size), jnp.bfloat16),
            pltpu.VMEM((head_size, length), jnp.float32),
            pltpu.VMEM((head_size, length), jnp.float32),
            pltpu.VMEM((2, length, head_size), jnp.bfloat16),
            pltpu.VMEM((head_size, width), jnp.float32),
            pltpu.VMEM((head_size, width), jnp.bfloat16),
            pltpu.VMEM((head_size, width), jnp.float32),
            pltpu.VMEM((SIDE, 2 * rows, width), jnp.bfloat16),
            pltpu.VMEM((2, rows, width), jnp.bfloat16),
            pltpu.VMEM((2, rows, width), jnp.bfloat16),
            pltpu.VMEM((head_size, width), jnp.bfloat16),
            pltpu.VMEM((rows, width), jnp.float32),
            pltpu.VMEM((head_size, width), jnp.bfloat16),
            pltpu.VMEM((head_size, width), jnp.bfloat16),
            pltpu.VMEM((head_size, width), jnp.float32),
            dma((3,)), dma((BLOCKS,)), dma((BLOCKS,)),
            dma((34,)), dma((34,)),
            dma((BLOCKS,)), dma((BLOCKS,)),
            dma((2,)), dma((3,)),
            dma((BLOCKS,)), dma((BLOCKS,)),
            dma((BLOCKS,)), dma((BLOCKS,)),
            dma((3,)), dma((3,)),
            dma((SIDE - 1,)), dma((SIDE - 1,)),
            dma((2,)), dma((2,)),
            dma((WORKERS - 1,)), dma((WORKERS - 1,)),
            dma((9,)),
        ],
        compiler_params=pltpu.CompilerParams(
            collective_id=0, has_side_effects=True, vmem_limit_bytes=56 << 20
        ),
    )(qkv[:, 0], d_out[0], w_out[0], tile_mask, momentum[0])
    grad_qkv, synced, worker_error, server_error = pl.pallas_call(
        finish,
        out_shape=(
            jax.ShapeDtypeStruct((3, tokens, HEADS, head_size), jnp.bfloat16),
            jax.ShapeDtypeStruct((head_size, width), jnp.bfloat16),
            jax.ShapeDtypeStruct((head_size, width), jnp.float32),
            jax.ShapeDtypeStruct((rows, width), jnp.float32),
        ),
        in_specs=[hbm] * 4,
        out_specs=(hbm,) * 4,
        scratch_shapes=[
            pltpu.VMEM((3, HEADS, tokens, head_size), jnp.bfloat16),
            pltpu.VMEM((3, tokens, HEADS, head_size), jnp.bfloat16),
            pltpu.VMEM((head_size, width), jnp.bfloat16),
            pltpu.VMEM((head_size, width), jnp.float32),
            pltpu.VMEM((rows, width), jnp.float32),
            dma((6,)), dma((6,)),
        ],
        compiler_params=pltpu.CompilerParams(vmem_limit_bytes=56 << 20),
    )(grads, synced, worker_error, server_error)
    grad_qkv = grad_qkv[:, None]
    return (grad_qkv, synced[None], worker_error[None, None], server_error[None])


def solution(mesh):
    placed = (
        P(None, "dp", "seq", None, None),
        P(),
        P("dp", "seq", None),
        P("seq", None, None),
        P("seq", None, None),
    )
    return jax.shard_map(
        body,
        mesh=mesh,
        in_specs=placed,
        out_specs=(
            P(None, "dp", "seq", None, None),
            P("seq", None, None),
            P("dp", "seq", None, None),
            P("seq", "dp", None),
        ),
        check_vma=False,
    )
```

```python
import functools
import math

import jax
import jax.numpy as jnp
from jax import lax
from jax.experimental import pallas as pl
from jax.experimental.pallas import tpu as pltpu
from jax.sharding import PartitionSpec as P

HEADS = 16
GROUPS = 8
TILE = 128
SIDE = 4
BLOCKS = SIDE * SIDE
WORKERS = 8
HALF = TILE // 2
PART = HALF // 2
MESH = pl.DeviceIdType.MESH

ORDER = (
    (0, 0), (0, 1), (0, 2), (0, 3),
    (-1, 0), (-1, 1), (1, 0), (1, 1),
    (2, 0), (2, 1),
    (-1, 2), (-1, 3), (1, 2), (1, 3),
    (2, 2), (2, 3),
)
OFFSETS = (0, -1, 1, 2)


def wrap(position, offset):
    return lax.rem(position + (offset + SIDE), SIDE)


def pick(step, table):
    value = jnp.int32(table[0])
    for index, entry in enumerate(table):
        if index and entry != table[0]:
            value = jnp.where(step == index, jnp.int32(entry), value)
    return value


def nt(a, b):
    return lax.dot_general(a, b, (((1,), (1,)), ((), ())), preferred_element_type=jnp.float32)


def nn(a, b):
    return lax.dot_general(a, b, (((1,), (0,)), ((), ())), preferred_element_type=jnp.float32)


def tn(a, b):
    return lax.dot_general(a, b, (((0,), (0,)), ((), ())), preferred_element_type=jnp.float32)


class Gather:
    def __init__(self, buf, z, columns, row0, send, recv):
        self.buf, self.z, self.columns, self.row0 = buf, z, columns, row0
        self.send, self.recv = send, recv

    def block(self, dz, column):
        return wrap(self.z, dz) * SIDE + self.columns[column]

    def copy(self, slot, block, lo, n, dz, column):
        rows = self.buf.at[block, pl.ds(pl.multiple_of(self.row0 + lo, PART // 2), n)]
        return pltpu.make_async_remote_copy(
            src_ref=rows,
            dst_ref=rows,
            send_sem=self.send.at[slot],
            recv_sem=self.recv.at[slot],
            device_id={"seq": self.block(dz, column)},
            device_id_type=MESH,
        )

    def ring(self, slot, column, kind, lo):
        if kind == 0:
            return self.copy(slot, self.block(0, column), lo, PART, 1, 0)
        if kind == 1:
            return self.copy(slot, self.block(0, column), lo, PART, -1, 0)
        if kind == 2:
            return self.copy(slot, self.block(-1, column), lo, PART // 2, 1, 0)
        return self.copy(slot, self.block(1, column), lo + PART // 2, PART // 2, -1, 0)

    def az(self, column, kind):
        return self.ring(column * 4 + kind, column, kind, 0)

    def ay(self, dz, column):
        slot = 8 + OFFSETS.index(dz) * 2 + column
        return self.copy(slot, self.block(dz, column), 0, PART, 0, 2)

    def by(self, column):
        return self.copy(16 + column, self.block(0, column), PART, PART, 0, 2)

    def bz(self, column, kind):
        return self.ring(18 + column * 4 + kind, column, kind, PART)

    def every(self):
        copies = [self.az(c, kind) for c in range(2) for kind in range(4)]
        copies += [self.ay(dz, c) for dz in OFFSETS for c in range(2)]
        copies += [self.by(c) for c in range(2)]
        return copies + [self.bz(c, kind) for c in range(4) for kind in range(4)]


def kernel(
    inv_root,
    qkv_ref, dout_ref, w_hbm, mask_ref, mom_hbm,
    grads_ref, sync_ref, werr_ref, serr_ref,
    gland, tokenwise, headwise, qkvbuf, dbuf, w_ref, mom_ref, bias, dqbuf, dkt, dvt, kvbuf, gw_ref,
    sentbuf, werrbuf, landed, parts, sums, syncbuf, serrbuf, gwout, gwin, jobmom,
    q_in, q_send, q_recv, d_send, d_recv, f_send, f_recv, i_send, i_recv,
    g_send, g_recv, kv_send, kv_recv, x_send, x_recv,
    m_send, m_recv, p_send, p_recv, s_send, s_recv, local_sem,
):
    me = lax.axis_index("seq")
    z = me // SIDE
    y = lax.rem(me, SIDE)
    worker = lax.axis_index("dp")
    x = worker // 2
    core = lax.rem(worker, 2)
    width = dout_ref.shape[1]
    rows = sentbuf.shape[0] // WORKERS

    side = y // 2
    home = core == side
    away = core != side
    columns = (y, 3 - y, y + 1 - 2 * lax.rem(y, 2), 2 - y + 2 * lax.rem(y, 2))
    other = x * 2 + 1 - core
    partner = z * SIDE + 3 - y
    head = jnp.where(home, me, partner)
    swap = {"dp": other, "seq": partner}
    slot_of_job = lax.rem(y, 2) * 2 + core

    own_d = pltpu.make_async_copy(dout_ref, dbuf.at[me], local_sem.at[0])
    all_q = [pltpu.make_async_copy(qkv_ref.at[p], tokenwise.at[p], q_in.at[p]) for p in range(3)]
    for copy in all_q:
        copy.start()
    own_q = pltpu.make_async_copy(
        headwise.at[:, me], qkvbuf.at[:, pl.ds(me * TILE, TILE)], local_sem.at[1]
    )
    own_w = pltpu.make_async_copy(w_hbm, w_ref, local_sem.at[2])
    own_m = pltpu.make_async_copy(mom_hbm, mom_ref, local_sem.at[3])
    home_m = pltpu.make_async_copy(mom_hbm, jobmom, local_sem.at[3])

    @pl.when(home)
    def _():
        own_d.start()
        own_w.start()
        home_m.start()

    pl.when(away)(own_m.start)

    workers = [
        wrap(x, dx) * 2 + lax.rem(core + dc, 2)
        for dx in (2, 1, -1, 0) for dc in range(2) if (dx, dc) != (0, 0)
    ]
    plane = [
        (x * 2 + lax.rem(core + dc, 2), wrap(z, dz) * SIDE + wrap(y, dy))
        for dc in range(2) for dz in range(SIDE) for dy in range(SIDE) if (dc, dz, dy) != (0, 0, 0)
    ]
    barrier = pltpu.get_barrier_semaphore()
    for dp, seq in plane:
        pl.semaphore_signal(
            barrier, inc=1, device_id={"dp": dp, "seq": seq}, device_id_type=MESH
        )
    for peer in workers[:-1]:
        pl.semaphore_signal(barrier, inc=1, device_id={"dp": peer}, device_id_type=MESH)
    pl.semaphore_wait(barrier, len(plane) + len(workers) - 1)

    starts = []
    for h in range(2):
        at = pl.ds(h * HALF, HALF)
        copy = pltpu.make_async_remote_copy(
            src_ref=dout_ref.at[at],
            dst_ref=dbuf.at[me, at],
            send_sem=i_send.at[h],
            recv_sem=i_recv.at[jnp.where(home, h, 2)],
            device_id={
                "dp": jnp.where(home, other, x * 2 + h),
                "seq": jnp.where(home, me, partner),
            },
            device_id_type=MESH,
        )
        copy.start()
        starts.append(copy)

    def landing(slot):
        at = pl.ds(0, HALF)
        return pltpu.make_async_remote_copy(
            src_ref=dout_ref.at[at],
            dst_ref=dbuf.at[me, at],
            send_sem=i_send.at[0],
            recv_sem=i_recv.at[slot],
            device_id=swap,
            device_id_type=MESH,
        )

    w_copy = pltpu.make_async_remote_copy(
        src_ref=w_hbm, dst_ref=w_ref, send_sem=x_send.at[0], recv_sem=x_recv.at[0],
        device_id=swap, device_id_type=MESH,
    )
    pl.when(away)(w_copy.start)

    def q_copy(dz, u, c, recv):
        z2, y2 = wrap(z, dz), 2 * core + u
        theirs = z2 * SIDE + jnp.where(core == c, y2, 3 - y2)
        return pltpu.make_async_remote_copy(
            src_ref=headwise.at[:, theirs],
            dst_ref=qkvbuf.at[:, pl.ds(me * TILE, TILE)],
            send_sem=q_send.at[dz * 4 + u * 2 + c],
            recv_sem=q_recv.at[recv],
            device_id={"dp": x * 2 + c, "seq": z2 * SIDE + y2},
            device_id_type=MESH,
        )

    def q_mine(dz, u, c):
        return (2 * core + u == y) & (core == c) if dz == 0 else None

    def unless(mine, action):
        if mine is None:
            action()
        else:
            pl.when(jnp.logical_not(mine))(action)

    q_keys = [(dz, u, c) for dz in range(SIDE) for u in range(2) for c in range(2)]
    gather = Gather(dbuf, z, columns, core * HALF, d_send, d_recv)

    def launch(column):
        gather.by(column).start()
        gather.az(column, 0).start()
        gather.az(column, 1).start()
        gather.ay(0, column).start()
        gather.bz(column, 0).start()
        gather.bz(column, 1).start()

    def block_of(step):
        column = pick(step, [o[1] for o in ORDER])
        base = jnp.where(column < 2, columns[0], columns[2])
        return wrap(z, pick(step, [o[0] for o in ORDER])) * SIDE + jnp.where(
            lax.rem(column, 2) == 0, base, 3 - base
        )

    def forward(step, block):
        at = dbuf.at[block, pl.ds(pl.multiple_of(core * HALF, HALF), HALF)]
        return pltpu.make_async_remote_copy(
            src_ref=at, dst_ref=at, send_sem=f_send.at[step], recv_sem=f_recv.at[step],
            device_id={"dp": other}, device_id_type=MESH,
        )

    def pass_on(dz, column):
        forward(ORDER.index((dz, column)), gather.block(dz, column)).start()

    @pl.when(home)
    def _():
        own_d.wait()
        launch(0)

    for p in range(3):
        all_q[p].wait()
        headwise[p] = jnp.swapaxes(tokenwise[p], 0, 1)
    for key in q_keys:
        unless(q_mine(*key), q_copy(*key, key[0] * 4 + y).start)
    pl.when(home)(own_q.start)

    @pl.when(away)
    def _():
        landing(core).wait_recv()
        launch(0)

    landing(2).wait_recv()
    launch(1)
    pass_on(0, 1)

    tiles = mask_ref[head // (HEADS // GROUPS)]
    for j in range(BLOCKS):
        bias[:, j * TILE:(j + 1) * TILE] = jnp.broadcast_to(
            jnp.where(tiles[:, j:j + 1] > 0, 0.0, -jnp.inf), (BLOCKS, TILE)
        )
    dkt[...] = jnp.zeros_like(dkt)
    dvt[...] = jnp.zeros_like(dvt)
    gw_ref[...] = jnp.zeros_like(gw_ref)

    for column in range(2):
        gather.az(column, 0).wait_recv()
        gather.az(column, 2).start()
        gather.ay(-1, column).start()
        gather.az(column, 1).wait_recv()
        gather.az(column, 3).start()
        gather.ay(1, column).start()
    for column in range(2):
        gather.by(column).wait_recv()
        gather.bz(column + 2, 0).start()
        gather.bz(column + 2, 1).start()

    pl.when(home)(home_m.wait)
    pl.when(away)(own_m.wait)
    pl.when(away)(landing(1 - core).wait_recv)
    pl.when(home)(own_q.wait)
    pl.when(home)(own_w.wait)
    pl.when(away)(w_copy.wait_recv)
    for dz in range(SIDE):
        for source in range(SIDE):
            unless((y == source) & home if dz == 0 else None,
                   q_copy(dz, 0, 0, dz * 4 + source).wait_recv)

    mom_copy = pltpu.make_async_remote_copy(
        src_ref=mom_hbm, dst_ref=jobmom, send_sem=x_send.at[2], recv_sem=x_recv.at[2],
        device_id=swap, device_id_type=MESH,
    )
    pl.when(away)(mom_copy.start)

    def arrive(step):
        if step == 2:
            for column in range(2):
                gather.ay(0, column).wait_recv()
                pass_on(0, column + 2)
        elif step == 4:
            for column in range(2):
                gather.az(column, 2).wait_recv()
                gather.az(column, 3).wait_recv()
                gather.ay(2, column).start()
            for column in range(2):
                gather.bz(column, 0).wait_recv()
                gather.bz(column, 2).start()
                pass_on(-1, column)
                gather.bz(column, 1).wait_recv()
                gather.bz(column, 3).start()
                pass_on(1, column)
        elif step == 8:
            for column in range(2):
                gather.bz(column, 2).wait_recv()
                gather.bz(column, 3).wait_recv()
                pass_on(2, column)
            for column in range(2, 4):
                gather.bz(column, 0).wait_recv()
                gather.bz(column, 2).start()
                gather.bz(column, 1).wait_recv()
                gather.bz(column, 3).start()
        elif step == 10:
            for column in range(2):
                gather.ay(-1, column).wait_recv()
                pass_on(-1, column + 2)
        elif step == 12:
            for column in range(2):
                gather.ay(1, column).wait_recv()
                pass_on(1, column + 2)
        elif step == 14:
            for column in range(2):
                gather.bz(column + 2, 2).wait_recv()
                gather.bz(column + 2, 3).wait_recv()
                gather.ay(2, column).wait_recv()
                pass_on(2, column + 2)

    def dq_copy(step, block, recv):
        return pltpu.make_async_remote_copy(
            src_ref=dqbuf.at[pl.ds(pl.multiple_of(block * TILE, TILE), TILE)],
            dst_ref=gland.at[0, head],
            send_sem=g_send.at[step],
            recv_sem=g_recv.at[recv],
            device_id={"dp": x * 2 + side, "seq": block},
            device_id_type=MESH,
        )

    def load(ref, blocks):
        return jnp.concatenate(
            [ref[pl.ds(pl.multiple_of(b * TILE, TILE), TILE), :] for b in blocks], axis=0
        )

    def body(turn, carry):
        for number in (2, 4, 8, 10, 12, 14):
            @pl.when(turn * 2 + 2 == number)
            def _():
                arrive(number)

        steps = (turn * 2, turn * 2 + 1)
        blocks = [block_of(step) for step in steps]
        pl.when(turn > 0)(forward(steps[0], blocks[0]).wait_recv)
        forward(steps[1], blocks[1]).wait_recv()
        q = load(qkvbuf.at[0], blocks)
        k = qkvbuf[1]
        v = qkvbuf[2]
        d = jnp.concatenate([dbuf[b] for b in blocks], axis=0)
        cot = nt(d, w_ref[...]).astype(jnp.bfloat16)
        hidden = jnp.concatenate(
            [jnp.broadcast_to(bias[pl.ds(b, 1), :], (TILE, bias.shape[1])) for b in blocks], axis=0
        )
        scores = nt(q, k) * inv_root + hidden
        top = jnp.max(scores, axis=-1, keepdims=True)
        expo = jnp.exp(scores - top)
        probs = expo * (1.0 / jnp.sum(expo, axis=-1, keepdims=True))
        probs_b = probs.astype(jnp.bfloat16)
        att = nn(probs_b, v).astype(jnp.bfloat16)
        delta = jnp.sum(
            cot.astype(jnp.float32) * att.astype(jnp.float32), axis=-1, keepdims=True
        )
        dscores = (probs * (nt(cot, v) - delta)).astype(jnp.bfloat16)
        dq = (nn(dscores, k) * inv_root).astype(jnp.bfloat16)
        for index, block in enumerate(blocks):
            dqbuf[pl.ds(pl.multiple_of(block * TILE, TILE), TILE), :] = (
                dq[index * TILE:(index + 1) * TILE]
            )
        for step, block in zip(steps, blocks):
            hop = lax.rem(pick(step, [o[0] for o in ORDER]) + SIDE, SIDE)
            pl.when((step > 0) | away)(dq_copy(step, block, hop * 4 + slot_of_job).start)

        dkt[...] += tn(q, dscores)
        dvt[...] += tn(cot, probs_b)
        gw_ref[...] += tn(att, d)
        return carry

    lax.fori_loop(0, BLOCKS // 2, body, 0)

    gw_copy = pltpu.make_async_remote_copy(
        src_ref=gwout, dst_ref=gwin, send_sem=x_send.at[1], recv_sem=x_recv.at[1],
        device_id=swap, device_id_type=MESH,
    )

    def rows_at(index):
        return pl.ds(pl.multiple_of(index * rows, rows), rows)

    def compress_all(mom, grad, sent):
        def moment(index, total):
            at = rows_at(index)
            value = 0.9 * mom[at, :] + 0.1 * grad[at, :].astype(jnp.float32)
            mom[at, :] = value
            return total + jnp.abs(value)

        total = lax.fori_loop(0, WORKERS, moment, jnp.zeros((rows, width), jnp.float32))
        scale = jnp.sum(total, axis=(0, 1), keepdims=True) / (rows * WORKERS * width) + 1e-06
        unscale = 1.0 / scale

        def compress(index, carry):
            at = rows_at(index)
            value = mom[at, :]
            code = (scale * jnp.tanh(value * unscale)).astype(jnp.bfloat16)
            if sent is not None:
                sent[at, :] = code
            werrbuf[at, :] = value - code.astype(jnp.float32)
            return carry

        lax.fori_loop(0, WORKERS, compress, 0)

    kvbuf[0] = (dkt[...] * inv_root).astype(jnp.bfloat16).T
    kvbuf[1] = dvt[...].astype(jnp.bfloat16).T

    def kv_copy(dz, target, recv):
        block = wrap(z, dz) * SIDE + target
        return pltpu.make_async_remote_copy(
            src_ref=kvbuf.at[:, pl.ds(pl.multiple_of(block * TILE, TILE), TILE)],
            dst_ref=gland.at[pl.ds(1, 2), head],
            send_sem=kv_send.at[dz * 4 + target],
            recv_sem=kv_recv.at[recv],
            device_id={"dp": x * 2 + side, "seq": block},
            device_id_type=MESH,
        )

    def kv_mine(dz, target):
        return (y == target) & home if dz == 0 else None

    kv_keys = [(dz, target) for dz in (2, 1, 3, 0) for target in range(SIDE)]
    for key in kv_keys:
        unless(kv_mine(*key), kv_copy(*key, key[0] * 4 + slot_of_job).start)
    own_kv = pltpu.make_async_copy(
        kvbuf.at[:, pl.ds(pl.multiple_of(me * TILE, TILE), TILE)],
        gland.at[pl.ds(1, 2), me],
        local_sem.at[5],
    )
    own_dq = pltpu.make_async_copy(
        dqbuf.at[pl.ds(pl.multiple_of(me * TILE, TILE), TILE)], gland.at[0, me], local_sem.at[6]
    )

    @pl.when(home)
    def _():
        own_kv.start()
        own_dq.start()

    gwout[...] = gw_ref[...].astype(jnp.bfloat16)

    @pl.when(away)
    def _():
        mom_copy.wait_recv()

    compress_all(jobmom, gwout, sentbuf)

    turns = (2, 1, 3)

    def pair(index):
        return pl.ds(pl.multiple_of(index * 2 * rows, 2 * rows), 2 * rows)

    m_copies = []
    for index, dx in enumerate(turns):
        copy = pltpu.make_async_remote_copy(
            src_ref=sentbuf.at[pair(wrap(x, dx))],
            dst_ref=landed.at[x],
            send_sem=m_send.at[index],
            recv_sem=m_recv.at[index],
            device_id={"dp": wrap(x, dx) * 2 + core},
            device_id_type=MESH,
        )
        copy.start()
        m_copies.append(copy)
    landed[x] = sentbuf[pair(x), :]
    werr_out = pltpu.make_async_copy(werrbuf, werr_ref, local_sem.at[4])
    pl.when(home)(werr_out.start)

    g_out = [
        pltpu.make_async_copy(tokenwise.at[p], grads_ref.at[p], q_in.at[p]) for p in range(3)
    ]
    pl.when(home)(own_dq.wait)
    for slot in range(BLOCKS):
        mine = home & (slot_of_job == slot) if slot < 4 else None
        unless(mine, dq_copy(0, me, slot).wait_recv)
    tokenwise[0] = jnp.swapaxes(gland[0], 0, 1)
    g_out[0].start()

    for copy in m_copies:
        copy.wait_recv()
    partial = landed[0].astype(jnp.float32)
    for index in range(1, SIDE):
        partial = partial + landed[index].astype(jnp.float32)
    partial = partial.astype(jnp.bfloat16)
    parts[0] = partial[:rows]
    parts[1] = partial[rows:]

    def part_copy(c, recv, seq):
        return pltpu.make_async_remote_copy(
            src_ref=parts.at[c],
            dst_ref=sums.at[recv],
            send_sem=p_send.at[c],
            recv_sem=p_recv.at[recv],
            device_id={"dp": x * 2 + c, "seq": seq},
            device_id_type=MESH,
        )

    @pl.when(home)
    def _():
        part_copy(1 - core, 0, me).start()
        sums[0] = parts[core]

    @pl.when(away)
    def _():
        part_copy(0, 1, partner).start()
        part_copy(1, 1, partner).start()
        gw_copy.start()
        part_copy(0, 0, me).wait_recv()

    part_copy(0, 1, partner).wait_recv()

    average = (sums[0].astype(jnp.float32) + sums[1].astype(jnp.float32)) / WORKERS
    server = jnp.sum(jnp.abs(average), axis=(0, 1), keepdims=True) / (rows * width) + 1e-06
    code = (server * jnp.tanh(average * (1.0 / server))).astype(jnp.bfloat16)
    syncbuf[rows_at(worker), :] = code
    serrbuf[...] = average - code.astype(jnp.float32)

    def sync_copy(slot, index, dp):
        at = syncbuf.at[rows_at(index)]
        return pltpu.make_async_remote_copy(
            src_ref=at, dst_ref=at, send_sem=s_send.at[slot], recv_sem=s_recv.at[slot],
            device_id={"dp": dp}, device_id_type=MESH,
        )

    for slot, dx in enumerate(turns):
        sync_copy(slot, worker, wrap(x, dx) * 2 + core).start()
    sync_copy(3, worker, other).start()
    serr_out = pltpu.make_async_copy(serrbuf, serr_ref, local_sem.at[8])
    serr_out.start()

    pl.when(home)(own_kv.wait)
    for slot in range(BLOCKS):
        mine = home & (slot_of_job == slot) if slot < 4 else None
        unless(mine, kv_copy(0, 0, slot).wait_recv)
    for p in range(1, 3):
        tokenwise[p] = jnp.swapaxes(gland[p], 0, 1)
        g_out[p].start()

    @pl.when(away)
    def _():
        gw_copy.wait_recv()
        compress_all(mom_ref, gwin, None)
        werr_out.start()

    for slot, dx in enumerate(turns):
        sync_copy(slot, worker, other).wait_recv()
        sync_copy(4 + slot, wrap(x, -dx) * 2 + core, other).start()
    for slot in range(3, 7):
        sync_copy(slot, worker, other).wait_recv()
    own_s = pltpu.make_async_copy(syncbuf, sync_ref, local_sem.at[7])
    own_s.start()

    for key in q_keys:
        unless(q_mine(*key), q_copy(*key, 0).wait_send)
    for copy in gather.every() + starts + m_copies:
        copy.wait_send()
    for slot in range(7):
        sync_copy(slot, worker, other).wait_send()

    @pl.when(home)
    def _():
        part_copy(1 - core, 0, me).wait_send()

    @pl.when(away)
    def _():
        part_copy(0, 1, partner).wait_send()
        part_copy(1, 1, partner).wait_send()
        w_copy.wait_send()
        mom_copy.wait_send()
        gw_copy.wait_send()

    for step in range(1, BLOCKS):
        forward(step, me).wait_send()

    for step in range(BLOCKS):
        unless(home if step == 0 else None, dq_copy(step, me, 0).wait_send)
    for key in kv_keys:
        unless(kv_mine(*key), kv_copy(*key, 0).wait_send)
    for copy in [own_s, werr_out, serr_out] + g_out:
        copy.wait()


def finish(
    grads_in, sync_in, werr_in, serr_in, grads_out, sync_out, werr_out, serr_out,
    grads, sync, werr, serr, in_sem, out_sem,
):
    loads, stores = [], []
    chunks = [(grads_in, grads, grads_out, p, 1) for p in range(3)]
    rows = werr.shape[0] // 2
    for half in range(2):
        chunks.append((werr_in, werr, werr_out, half * rows, rows))
    chunks.append((sync_in, sync, sync_out, 0, sync.shape[0]))
    chunks.append((serr_in, serr, serr_out, 0, serr.shape[0]))
    for index, (source, buf, target, first, count) in enumerate(chunks):
        at = pl.ds(first, count)
        loads.append(pltpu.make_async_copy(source.at[at], buf.at[at], in_sem.at[index]))
        stores.append(pltpu.make_async_copy(buf.at[at], target.at[at], out_sem.at[index]))
    for load in loads:
        load.start()
    for load, store in zip(loads, stores):
        load.wait()
        store.start()
    for store in stores:
        store.wait()


def body(qkv, tile_mask, d_out, w_out, momentum):
    tokens, head_size = qkv.shape[2], qkv.shape[4]
    width = d_out.shape[2]
    length = tokens * BLOCKS
    inv_root = 1.0 / math.sqrt(head_size)
    rows = head_size // WORKERS
    vmem = pl.BlockSpec(memory_space=pltpu.VMEM)
    hbm = pl.BlockSpec(memory_space=pl.ANY)
    dma = pltpu.SemaphoreType.DMA
    grads, synced, worker_error, server_error = pl.pallas_call(
        functools.partial(kernel, inv_root),
        out_shape=(
            jax.ShapeDtypeStruct((3, tokens, HEADS, head_size), jnp.bfloat16),
            jax.ShapeDtypeStruct((head_size, width), jnp.bfloat16),
            jax.ShapeDtypeStruct((head_size, width), jnp.float32),
            jax.ShapeDtypeStruct((rows, width), jnp.float32),
        ),
        in_specs=[hbm, hbm, hbm, vmem, hbm],
        out_specs=(hbm, hbm, hbm, hbm),
        scratch_shapes=[
            pltpu.VMEM((3, HEADS, tokens, head_size), jnp.bfloat16),
            pltpu.VMEM((3, tokens, HEADS, head_size), jnp.bfloat16),
            pltpu.VMEM((3, HEADS, tokens, head_size), jnp.bfloat16),
            pltpu.VMEM((3, length, head_size), jnp.bfloat16),
            pltpu.VMEM((BLOCKS, tokens, width), jnp.bfloat16),
            pltpu.VMEM((head_size, width), jnp.bfloat16),
            pltpu.VMEM((head_size, width), jnp.float32),
            pltpu.VMEM((BLOCKS, length), jnp.float32),
            pltpu.VMEM((length, head_size), jnp.bfloat16),
            pltpu.VMEM((head_size, length), jnp.float32),
            pltpu.VMEM((head_size, length), jnp.float32),
            pltpu.VMEM((2, length, head_size), jnp.bfloat16),
            pltpu.VMEM((head_size, width), jnp.float32),
            pltpu.VMEM((head_size, width), jnp.bfloat16),
            pltpu.VMEM((head_size, width), jnp.float32),
            pltpu.VMEM((SIDE, 2 * rows, width), jnp.bfloat16),
            pltpu.VMEM((2, rows, width), jnp.bfloat16),
            pltpu.VMEM((2, rows, width), jnp.bfloat16),
            pltpu.VMEM((head_size, width), jnp.bfloat16),
            pltpu.VMEM((rows, width), jnp.float32),
            pltpu.VMEM((head_size, width), jnp.bfloat16),
            pltpu.VMEM((head_size, width), jnp.bfloat16),
            pltpu.VMEM((head_size, width), jnp.float32),
            dma((3,)), dma((BLOCKS,)), dma((BLOCKS,)),
            dma((34,)), dma((34,)),
            dma((BLOCKS,)), dma((BLOCKS,)),
            dma((2,)), dma((3,)),
            dma((BLOCKS,)), dma((BLOCKS,)),
            dma((BLOCKS,)), dma((BLOCKS,)),
            dma((3,)), dma((3,)),
            dma((SIDE - 1,)), dma((SIDE - 1,)),
            dma((2,)), dma((2,)),
            dma((WORKERS - 1,)), dma((WORKERS - 1,)),
            dma((9,)),
        ],
        compiler_params=pltpu.CompilerParams(
            collective_id=0, has_side_effects=True, vmem_limit_bytes=56 << 20
        ),
    )(qkv[:, 0], d_out[0], w_out[0], tile_mask, momentum[0])
    grad_qkv, synced, worker_error, server_error = pl.pallas_call(
        finish,
        out_shape=(
            jax.ShapeDtypeStruct((3, tokens, HEADS, head_size), jnp.bfloat16),
            jax.ShapeDtypeStruct((head_size, width), jnp.bfloat16),
            jax.ShapeDtypeStruct((head_size, width), jnp.float32),
            jax.ShapeDtypeStruct((rows, width), jnp.float32),
        ),
        in_specs=[hbm] * 4,
        out_specs=(hbm,) * 4,
        scratch_shapes=[
            pltpu.VMEM((3, tokens, HEADS, head_size), jnp.bfloat16),
            pltpu.VMEM((head_size, width), jnp.bfloat16),
            pltpu.VMEM((head_size, width), jnp.float32),
            pltpu.VMEM((rows, width), jnp.float32),
            dma((7,)), dma((7,)),
        ],
        compiler_params=pltpu.CompilerParams(vmem_limit_bytes=56 << 20),
    )(grads, synced, worker_error, server_error)
    grad_qkv = grad_qkv[:, None]
    return (grad_qkv, synced[None], worker_error[None, None], server_error[None])


def solution(mesh):
    placed = (
        P(None, "dp", "seq", None, None),
        P(),
        P("dp", "seq", None),
        P("seq", None, None),
        P("seq", None, None),
    )
    return jax.shard_map(
        body,
        mesh=mesh,
        in_specs=placed,
        out_specs=(
            P(None, "dp", "seq", None, None),
            P("seq", None, None),
            P("dp", "seq", None, None),
            P("seq", "dp", None),
        ),
        check_vma=False,
    )
```

```python
import functools
import math

import jax
import jax.numpy as jnp
from jax import lax
from jax.experimental import pallas as pl
from jax.experimental.pallas import tpu as pltpu
from jax.sharding import PartitionSpec as P

HEADS = 16
GROUPS = 8
TILE = 128
SIDE = 4
BLOCKS = SIDE * SIDE
WORKERS = 8
HALF = TILE // 2
PART = HALF // 2
MESH = pl.DeviceIdType.MESH

ORDER = (
    (0, 0), (0, 1), (0, 2), (0, 3),
    (-1, 0), (-1, 1), (1, 0), (1, 1),
    (2, 0), (2, 1),
    (-1, 2), (-1, 3), (1, 2), (1, 3),
    (2, 2), (2, 3),
)
OFFSETS = (0, -1, 1, 2)


def wrap(position, offset):
    return lax.rem(position + (offset + SIDE), SIDE)


def pick(step, table):
    value = jnp.int32(table[0])
    for index, entry in enumerate(table):
        if index and entry != table[0]:
            value = jnp.where(step == index, jnp.int32(entry), value)
    return value


def nt(a, b):
    return lax.dot_general(a, b, (((1,), (1,)), ((), ())), preferred_element_type=jnp.float32)


def nn(a, b):
    return lax.dot_general(a, b, (((1,), (0,)), ((), ())), preferred_element_type=jnp.float32)


def tn(a, b):
    return lax.dot_general(a, b, (((0,), (0,)), ((), ())), preferred_element_type=jnp.float32)


class Gather:
    def __init__(self, buf, z, columns, row0, send, recv):
        self.buf, self.z, self.columns, self.row0 = buf, z, columns, row0
        self.send, self.recv = send, recv

    def block(self, dz, column):
        return wrap(self.z, dz) * SIDE + self.columns[column]

    def copy(self, slot, block, lo, n, dz, column):
        rows = self.buf.at[block, pl.ds(pl.multiple_of(self.row0 + lo, PART // 2), n)]
        return pltpu.make_async_remote_copy(
            src_ref=rows,
            dst_ref=rows,
            send_sem=self.send.at[slot],
            recv_sem=self.recv.at[slot],
            device_id={"seq": self.block(dz, column)},
            device_id_type=MESH,
        )

    def ring(self, slot, column, kind, lo):
        if kind == 0:
            return self.copy(slot, self.block(0, column), lo, PART, 1, 0)
        if kind == 1:
            return self.copy(slot, self.block(0, column), lo, PART, -1, 0)
        if kind == 2:
            return self.copy(slot, self.block(-1, column), lo, PART // 2, 1, 0)
        return self.copy(slot, self.block(1, column), lo + PART // 2, PART // 2, -1, 0)

    def az(self, column, kind):
        return self.ring(column * 4 + kind, column, kind, 0)

    def ay(self, dz, column):
        slot = 8 + OFFSETS.index(dz) * 2 + column
        return self.copy(slot, self.block(dz, column), 0, PART, 0, 2)

    def by(self, column):
        return self.copy(16 + column, self.block(0, column), PART, PART, 0, 2)

    def bz(self, column, kind):
        return self.ring(18 + column * 4 + kind, column, kind, PART)

    def every(self):
        copies = [self.az(c, kind) for c in range(2) for kind in range(4)]
        copies += [self.ay(dz, c) for dz in OFFSETS for c in range(2)]
        copies += [self.by(c) for c in range(2)]
        return copies + [self.bz(c, kind) for c in range(4) for kind in range(4)]


def kernel(
    inv_root,
    qkv_ref, dout_ref, w_hbm, mask_ref, mom_hbm,
    grads_ref, sync_ref, werr_ref, serr_ref,
    gland, tokenwise, headwise, qkvbuf, dbuf, w_ref, mom_ref, bias, dqbuf, dkt, dvt, kvbuf, gw_ref,
    sentbuf, werrbuf, landed, parts, sums, syncbuf, serrbuf, gwout, gwin, jobmom,
    q_in, q_send, q_recv, d_send, d_recv, f_send, f_recv, i_send, i_recv,
    g_send, g_recv, kv_send, kv_recv, x_send, x_recv,
    m_send, m_recv, p_send, p_recv, s_send, s_recv, local_sem,
):
    me = lax.axis_index("seq")
    z = me // SIDE
    y = lax.rem(me, SIDE)
    worker = lax.axis_index("dp")
    x = worker // 2
    core = lax.rem(worker, 2)
    width = dout_ref.shape[1]
    rows = sentbuf.shape[0] // WORKERS

    side = y // 2
    home = core == side
    away = core != side
    columns = (y, 3 - y, y + 1 - 2 * lax.rem(y, 2), 2 - y + 2 * lax.rem(y, 2))
    other = x * 2 + 1 - core
    partner = z * SIDE + 3 - y
    head = jnp.where(home, me, partner)
    swap = {"dp": other, "seq": partner}
    slot_of_job = lax.rem(y, 2) * 2 + core

    own_d = pltpu.make_async_copy(dout_ref, dbuf.at[me], local_sem.at[0])
    all_q = [pltpu.make_async_copy(qkv_ref.at[p], tokenwise.at[p], q_in.at[p]) for p in range(3)]
    for copy in all_q:
        copy.start()
    own_q = pltpu.make_async_copy(
        headwise.at[:, me], qkvbuf.at[:, pl.ds(me * TILE, TILE)], local_sem.at[1]
    )
    own_w = pltpu.make_async_copy(w_hbm, w_ref, local_sem.at[2])
    own_m = pltpu.make_async_copy(mom_hbm, mom_ref, local_sem.at[3])
    home_m = pltpu.make_async_copy(mom_hbm, jobmom, local_sem.at[3])

    @pl.when(home)
    def _():
        own_d.start()
        own_w.start()
        home_m.start()

    pl.when(away)(own_m.start)

    workers = [
        wrap(x, dx) * 2 + lax.rem(core + dc, 2)
        for dx in (2, 1, -1, 0) for dc in range(2) if (dx, dc) != (0, 0)
    ]
    plane = [
        (x * 2 + lax.rem(core + dc, 2), wrap(z, dz) * SIDE + wrap(y, dy))
        for dc in range(2) for dz in range(SIDE) for dy in range(SIDE) if (dc, dz, dy) != (0, 0, 0)
    ]
    barrier = pltpu.get_barrier_semaphore()
    for dp, seq in plane:
        pl.semaphore_signal(
            barrier, inc=1, device_id={"dp": dp, "seq": seq}, device_id_type=MESH
        )
    for peer in workers[:-1]:
        pl.semaphore_signal(barrier, inc=1, device_id={"dp": peer}, device_id_type=MESH)
    for p in range(3):
        all_q[p].wait()
        headwise[p] = jnp.swapaxes(tokenwise[p], 0, 1)
    pl.semaphore_wait(barrier, len(plane) + len(workers) - 1)

    starts = []
    for h in range(2):
        at = pl.ds(h * HALF, HALF)
        copy = pltpu.make_async_remote_copy(
            src_ref=dout_ref.at[at],
            dst_ref=dbuf.at[me, at],
            send_sem=i_send.at[h],
            recv_sem=i_recv.at[jnp.where(home, h, 2)],
            device_id={
                "dp": jnp.where(home, other, x * 2 + h),
                "seq": jnp.where(home, me, partner),
            },
            device_id_type=MESH,
        )
        copy.start()
        starts.append(copy)

    def landing(slot):
        at = pl.ds(0, HALF)
        return pltpu.make_async_remote_copy(
            src_ref=dout_ref.at[at],
            dst_ref=dbuf.at[me, at],
            send_sem=i_send.at[0],
            recv_sem=i_recv.at[slot],
            device_id=swap,
            device_id_type=MESH,
        )

    w_copy = pltpu.make_async_remote_copy(
        src_ref=w_hbm, dst_ref=w_ref, send_sem=x_send.at[0], recv_sem=x_recv.at[0],
        device_id=swap, device_id_type=MESH,
    )

    def q_copy(dz, u, c, recv):
        z2, y2 = wrap(z, dz), 2 * core + u
        theirs = z2 * SIDE + jnp.where(core == c, y2, 3 - y2)
        return pltpu.make_async_remote_copy(
            src_ref=headwise.at[:, theirs],
            dst_ref=qkvbuf.at[:, pl.ds(me * TILE, TILE)],
            send_sem=q_send.at[dz * 4 + u * 2 + c],
            recv_sem=q_recv.at[recv],
            device_id={"dp": x * 2 + c, "seq": z2 * SIDE + y2},
            device_id_type=MESH,
        )

    def q_mine(dz, u, c):
        return (2 * core + u == y) & (core == c) if dz == 0 else None

    def unless(mine, action):
        if mine is None:
            action()
        else:
            pl.when(jnp.logical_not(mine))(action)

    q_keys = [(dz, u, c) for dz in range(SIDE) for u in range(2) for c in range(2)]
    gather = Gather(dbuf, z, columns, core * HALF, d_send, d_recv)

    def launch(column):
        gather.by(column).start()
        gather.az(column, 0).start()
        gather.az(column, 1).start()
        gather.ay(0, column).start()
        gather.bz(column, 0).start()
        gather.bz(column, 1).start()

    def block_of(step):
        column = pick(step, [o[1] for o in ORDER])
        base = jnp.where(column < 2, columns[0], columns[2])
        return wrap(z, pick(step, [o[0] for o in ORDER])) * SIDE + jnp.where(
            lax.rem(column, 2) == 0, base, 3 - base
        )

    def forward(step, block):
        at = dbuf.at[block, pl.ds(pl.multiple_of(core * HALF, HALF), HALF)]
        return pltpu.make_async_remote_copy(
            src_ref=at, dst_ref=at, send_sem=f_send.at[step], recv_sem=f_recv.at[step],
            device_id={"dp": other}, device_id_type=MESH,
        )

    def pass_on(dz, column):
        forward(ORDER.index((dz, column)), gather.block(dz, column)).start()

    @pl.when(home)
    def _():
        own_d.wait()
        launch(0)

    def send_q():
        for key in q_keys:
            unless(q_mine(*key), q_copy(*key, key[0] * 4 + y).start)

    @pl.when(home)
    def _():
        send_q()
        own_q.start()


    @pl.when(away)
    def _():
        landing(core).wait_recv()
        launch(0)

    landing(2).wait_recv()
    launch(1)
    pass_on(0, 1)

    @pl.when(away)
    def _():
        for copy in starts:
            copy.wait_send()
        w_copy.start()
        send_q()


    tiles = mask_ref[head // (HEADS // GROUPS)]
    for j in range(BLOCKS):
        bias[:, j * TILE:(j + 1) * TILE] = jnp.broadcast_to(
            jnp.where(tiles[:, j:j + 1] > 0, 0.0, -jnp.inf), (BLOCKS, TILE)
        )
    dkt[...] = jnp.zeros_like(dkt)
    dvt[...] = jnp.zeros_like(dvt)
    gw_ref[...] = jnp.zeros_like(gw_ref)

    for column in range(2):
        gather.az(column, 0).wait_recv()
        gather.az(column, 2).start()
        gather.ay(-1, column).start()
        gather.az(column, 1).wait_recv()
        gather.az(column, 3).start()
        gather.ay(1, column).start()
    for column in range(2):
        gather.by(column).wait_recv()
        gather.bz(column + 2, 0).start()
        gather.bz(column + 2, 1).start()

    pl.when(home)(home_m.wait)
    pl.when(away)(own_m.wait)
    pl.when(away)(landing(1 - core).wait_recv)
    pl.when(home)(own_q.wait)
    pl.when(home)(own_w.wait)
    pl.when(away)(w_copy.wait_recv)
    for dz in range(SIDE):
        for source in range(SIDE):
            unless((y == source) & home if dz == 0 else None,
                   q_copy(dz, 0, 0, dz * 4 + source).wait_recv)

    mom_copy = pltpu.make_async_remote_copy(
        src_ref=mom_hbm, dst_ref=jobmom, send_sem=x_send.at[2], recv_sem=x_recv.at[2],
        device_id=swap, device_id_type=MESH,
    )
    pl.when(away)(mom_copy.start)

    def arrive(step):
        if step == 2:
            for column in range(2):
                gather.ay(0, column).wait_recv()
                pass_on(0, column + 2)
        elif step == 4:
            for column in range(2):
                gather.az(column, 2).wait_recv()
                gather.az(column, 3).wait_recv()
                gather.ay(2, column).start()
            for column in range(2):
                gather.bz(column, 0).wait_recv()
                gather.bz(column, 2).start()
                pass_on(-1, column)
                gather.bz(column, 1).wait_recv()
                gather.bz(column, 3).start()
                pass_on(1, column)
        elif step == 8:
            for column in range(2):
                gather.bz(column, 2).wait_recv()
                gather.bz(column, 3).wait_recv()
                pass_on(2, column)
            for column in range(2, 4):
                gather.bz(column, 0).wait_recv()
                gather.bz(column, 2).start()
                gather.bz(column, 1).wait_recv()
                gather.bz(column, 3).start()
        elif step == 10:
            for column in range(2):
                gather.ay(-1, column).wait_recv()
                pass_on(-1, column + 2)
        elif step == 12:
            for column in range(2):
                gather.ay(1, column).wait_recv()
                pass_on(1, column + 2)
        elif step == 14:
            for column in range(2):
                gather.bz(column + 2, 2).wait_recv()
                gather.bz(column + 2, 3).wait_recv()
                gather.ay(2, column).wait_recv()
                pass_on(2, column + 2)

    def dq_copy(step, block, recv):
        return pltpu.make_async_remote_copy(
            src_ref=dqbuf.at[pl.ds(pl.multiple_of(block * TILE, TILE), TILE)],
            dst_ref=gland.at[0, head],
            send_sem=g_send.at[step],
            recv_sem=g_recv.at[recv],
            device_id={"dp": x * 2 + side, "seq": block},
            device_id_type=MESH,
        )

    def load(ref, blocks):
        return jnp.concatenate(
            [ref[pl.ds(pl.multiple_of(b * TILE, TILE), TILE), :] for b in blocks], axis=0
        )

    def body(turn, carry):
        for number in (2, 4, 8, 10, 12, 14):
            @pl.when(turn * 2 + 2 == number)
            def _():
                arrive(number)

        steps = (turn * 2, turn * 2 + 1)
        blocks = [block_of(step) for step in steps]
        pl.when(turn > 0)(forward(steps[0], blocks[0]).wait_recv)
        forward(steps[1], blocks[1]).wait_recv()
        q = load(qkvbuf.at[0], blocks)
        k = qkvbuf[1]
        v = qkvbuf[2]
        d = jnp.concatenate([dbuf[b] for b in blocks], axis=0)
        cot = nt(d, w_ref[...]).astype(jnp.bfloat16)
        hidden = jnp.concatenate(
            [jnp.broadcast_to(bias[pl.ds(b, 1), :], (TILE, bias.shape[1])) for b in blocks], axis=0
        )
        scores = nt(q, k) * inv_root + hidden
        top = jnp.max(scores, axis=-1, keepdims=True)
        expo = jnp.exp(scores - top)
        probs = expo * (1.0 / jnp.sum(expo, axis=-1, keepdims=True))
        probs_b = probs.astype(jnp.bfloat16)
        att = nn(probs_b, v).astype(jnp.bfloat16)
        delta = jnp.sum(
            cot.astype(jnp.float32) * att.astype(jnp.float32), axis=-1, keepdims=True
        )
        dscores = (probs * (nt(cot, v) - delta)).astype(jnp.bfloat16)
        dq = (nn(dscores, k) * inv_root).astype(jnp.bfloat16)
        for index, block in enumerate(blocks):
            dqbuf[pl.ds(pl.multiple_of(block * TILE, TILE), TILE), :] = (
                dq[index * TILE:(index + 1) * TILE]
            )
        for step, block in zip(steps, blocks):
            hop = lax.rem(pick(step, [o[0] for o in ORDER]) + SIDE, SIDE)
            pl.when((step > 0) | away)(dq_copy(step, block, hop * 4 + slot_of_job).start)

        dkt[...] += tn(q, dscores)
        dvt[...] += tn(cot, probs_b)
        gw_ref[...] += tn(att, d)
        return carry

    lax.fori_loop(0, BLOCKS // 2, body, 0)

    gw_copy = pltpu.make_async_remote_copy(
        src_ref=gwout, dst_ref=gwin, send_sem=x_send.at[1], recv_sem=x_recv.at[1],
        device_id=swap, device_id_type=MESH,
    )

    def rows_at(index):
        return pl.ds(pl.multiple_of(index * rows, rows), rows)

    def compress_all(mom, grad, sent):
        def moment(index, total):
            at = rows_at(index)
            value = 0.9 * mom[at, :] + 0.1 * grad[at, :].astype(jnp.float32)
            mom[at, :] = value
            return total + jnp.abs(value)

        total = lax.fori_loop(0, WORKERS, moment, jnp.zeros((rows, width), jnp.float32))
        scale = jnp.sum(total, axis=(0, 1), keepdims=True) / (rows * WORKERS * width) + 1e-06
        unscale = 1.0 / scale

        def compress(index, carry):
            at = rows_at(index)
            value = mom[at, :]
            code = (scale * jnp.tanh(value * unscale)).astype(jnp.bfloat16)
            if sent is not None:
                sent[at, :] = code
            werrbuf[at, :] = value - code.astype(jnp.float32)
            return carry

        lax.fori_loop(0, WORKERS, compress, 0)

    gw_copy = pltpu.make_async_remote_copy(
        src_ref=gwout, dst_ref=gwin, send_sem=x_send.at[1], recv_sem=x_recv.at[1],
        device_id=swap, device_id_type=MESH,
    )

    def rows_at(index):
        return pl.ds(pl.multiple_of(index * rows, rows), rows)

    def compress_all(mom, grad, sent):
        def moment(index, total):
            at = rows_at(index)
            value = 0.9 * mom[at, :] + 0.1 * grad[at, :].astype(jnp.float32)
            mom[at, :] = value
            return total + jnp.abs(value)

        total = lax.fori_loop(0, WORKERS, moment, jnp.zeros((rows, width), jnp.float32))
        scale = jnp.sum(total, axis=(0, 1), keepdims=True) / (rows * WORKERS * width) + 1e-06
        unscale = 1.0 / scale

        def compress(index, carry):
            at = rows_at(index)
            value = mom[at, :]
            code = (scale * jnp.tanh(value * unscale)).astype(jnp.bfloat16)
            if sent is not None:
                sent[at, :] = code
            werrbuf[at, :] = value - code.astype(jnp.float32)
            return carry

        lax.fori_loop(0, WORKERS, compress, 0)

    kvbuf[0] = (dkt[...] * inv_root).astype(jnp.bfloat16).T
    kvbuf[1] = dvt[...].astype(jnp.bfloat16).T

    def kv_copy(dz, target, recv):
        block = wrap(z, dz) * SIDE + target
        return pltpu.make_async_remote_copy(
            src_ref=kvbuf.at[:, pl.ds(pl.multiple_of(block * TILE, TILE), TILE)],
            dst_ref=gland.at[pl.ds(1, 2), head],
            send_sem=kv_send.at[dz * 4 + target],
            recv_sem=kv_recv.at[recv],
            device_id={"dp": x * 2 + side, "seq": block},
            device_id_type=MESH,
        )

    def kv_mine(dz, target):
        return (y == target) & home if dz == 0 else None

    kv_keys = [(dz, target) for dz in (2, 1, 3, 0) for target in range(SIDE)]
    for key in kv_keys:
        unless(kv_mine(*key), kv_copy(*key, key[0] * 4 + slot_of_job).start)
    own_kv = pltpu.make_async_copy(
        kvbuf.at[:, pl.ds(pl.multiple_of(me * TILE, TILE), TILE)],
        gland.at[pl.ds(1, 2), me],
        local_sem.at[5],
    )
    own_dq = pltpu.make_async_copy(
        dqbuf.at[pl.ds(pl.multiple_of(me * TILE, TILE), TILE)], gland.at[0, me], local_sem.at[6]
    )

    @pl.when(home)
    def _():
        own_kv.start()
        own_dq.start()

    gwout[...] = gw_ref[...].astype(jnp.bfloat16)

    @pl.when(away)
    def _():
        mom_copy.wait_recv()

    compress_all(jobmom, gwout, sentbuf)

    turns = (2, 1, 3)

    def pair(index):
        return pl.ds(pl.multiple_of(index * 2 * rows, 2 * rows), 2 * rows)

    m_copies = []
    for index, dx in enumerate(turns):
        copy = pltpu.make_async_remote_copy(
            src_ref=sentbuf.at[pair(wrap(x, dx))],
            dst_ref=landed.at[x],
            send_sem=m_send.at[index],
            recv_sem=m_recv.at[index],
            device_id={"dp": wrap(x, dx) * 2 + core},
            device_id_type=MESH,
        )
        copy.start()
        m_copies.append(copy)
    landed[x] = sentbuf[pair(x), :]
    werr_out = pltpu.make_async_copy(werrbuf, werr_ref, local_sem.at[4])
    pl.when(home)(werr_out.start)

    g_out = [
        pltpu.make_async_copy(tokenwise.at[p], grads_ref.at[p], q_in.at[p]) for p in range(3)
    ]
    pl.when(home)(own_dq.wait)
    for slot in range(BLOCKS):
        mine = home & (slot_of_job == slot) if slot < 4 else None
        unless(mine, dq_copy(0, me, slot).wait_recv)
    tokenwise[0] = jnp.swapaxes(gland[0], 0, 1)
    g_out[0].start()

    for copy in m_copies:
        copy.wait_recv()
    partial = landed[0].astype(jnp.float32)
    for index in range(1, SIDE):
        partial = partial + landed[index].astype(jnp.float32)
    partial = partial.astype(jnp.bfloat16)
    parts[0] = partial[:rows]
    parts[1] = partial[rows:]

    def part_copy(c, recv, seq):
        return pltpu.make_async_remote_copy(
            src_ref=parts.at[c],
            dst_ref=sums.at[recv],
            send_sem=p_send.at[c],
            recv_sem=p_recv.at[recv],
            device_id={"dp": x * 2 + c, "seq": seq},
            device_id_type=MESH,
        )

    @pl.when(home)
    def _():
        part_copy(1 - core, 0, me).start()
        sums[0] = parts[core]

    @pl.when(away)
    def _():
        part_copy(0, 1, partner).start()
        part_copy(1, 1, partner).start()
        gw_copy.start()
        part_copy(0, 0, me).wait_recv()

    part_copy(0, 1, partner).wait_recv()

    average = (sums[0].astype(jnp.float32) + sums[1].astype(jnp.float32)) / WORKERS
    server = jnp.sum(jnp.abs(average), axis=(0, 1), keepdims=True) / (rows * width) + 1e-06
    code = (server * jnp.tanh(average * (1.0 / server))).astype(jnp.bfloat16)
    syncbuf[rows_at(worker), :] = code
    serrbuf[...] = average - code.astype(jnp.float32)

    def sync_copy(slot, index, dp):
        at = syncbuf.at[rows_at(index)]
        return pltpu.make_async_remote_copy(
            src_ref=at, dst_ref=at, send_sem=s_send.at[slot], recv_sem=s_recv.at[slot],
            device_id={"dp": dp}, device_id_type=MESH,
        )

    for slot, dx in enumerate(turns):
        sync_copy(slot, worker, wrap(x, dx) * 2 + core).start()
    sync_copy(3, worker, other).start()
    serr_out = pltpu.make_async_copy(serrbuf, serr_ref, local_sem.at[8])
    serr_out.start()

    pl.when(home)(own_kv.wait)
    for slot in range(BLOCKS):
        mine = home & (slot_of_job == slot) if slot < 4 else None
        unless(mine, kv_copy(0, 0, slot).wait_recv)
    for p in range(1, 3):
        tokenwise[p] = jnp.swapaxes(gland[p], 0, 1)
        g_out[p].start()

    @pl.when(away)
    def _():
        gw_copy.wait_recv()
        compress_all(mom_ref, gwin, None)
        werr_out.start()

    for slot, dx in enumerate(turns):
        sync_copy(slot, worker, other).wait_recv()
        sync_copy(4 + slot, wrap(x, -dx) * 2 + core, other).start()
    for slot in range(3, 7):
        sync_copy(slot, worker, other).wait_recv()
    own_s = pltpu.make_async_copy(syncbuf, sync_ref, local_sem.at[7])
    own_s.start()

    for key in q_keys:
        unless(q_mine(*key), q_copy(*key, 0).wait_send)
    for copy in gather.every() + m_copies:
        copy.wait_send()

    @pl.when(home)
    def _():
        for copy in starts:
            copy.wait_send()

    for slot in range(7):
        sync_copy(slot, worker, other).wait_send()

    @pl.when(home)
    def _():
        part_copy(1 - core, 0, me).wait_send()

    @pl.when(away)
    def _():
        part_copy(0, 1, partner).wait_send()
        part_copy(1, 1, partner).wait_send()
        w_copy.wait_send()
        mom_copy.wait_send()
        gw_copy.wait_send()

    for step in range(1, BLOCKS):
        forward(step, me).wait_send()

    for step in range(BLOCKS):
        unless(home if step == 0 else None, dq_copy(step, me, 0).wait_send)
    for key in kv_keys:
        unless(kv_mine(*key), kv_copy(*key, 0).wait_send)
    for copy in [own_s, werr_out, serr_out] + g_out:
        copy.wait()


def finish(
    grads_in, sync_in, werr_in, serr_in, grads_out, sync_out, werr_out, serr_out,
    grads, sync, werr, serr, in_sem, out_sem,
):
    loads, stores = [], []
    chunks = [(grads_in, grads, grads_out, p, 1) for p in range(3)]
    rows = werr.shape[0] // 2
    for half in range(2):
        chunks.append((werr_in, werr, werr_out, half * rows, rows))
    chunks.append((sync_in, sync, sync_out, 0, sync.shape[0]))
    chunks.append((serr_in, serr, serr_out, 0, serr.shape[0]))
    for index, (source, buf, target, first, count) in enumerate(chunks):
        at = pl.ds(first, count)
        loads.append(pltpu.make_async_copy(source.at[at], buf.at[at], in_sem.at[index]))
        stores.append(pltpu.make_async_copy(buf.at[at], target.at[at], out_sem.at[index]))
    for load in loads:
        load.start()
    for load, store in zip(loads, stores):
        load.wait()
        store.start()
    for store in stores:
        store.wait()


def body(qkv, tile_mask, d_out, w_out, momentum):
    tokens, head_size = qkv.shape[2], qkv.shape[4]
    width = d_out.shape[2]
    length = tokens * BLOCKS
    inv_root = 1.0 / math.sqrt(head_size)
    rows = head_size // WORKERS
    vmem = pl.BlockSpec(memory_space=pltpu.VMEM)
    hbm = pl.BlockSpec(memory_space=pl.ANY)
    dma = pltpu.SemaphoreType.DMA
    grads, synced, worker_error, server_error = pl.pallas_call(
        functools.partial(kernel, inv_root),
        out_shape=(
            jax.ShapeDtypeStruct((3, tokens, HEADS, head_size), jnp.bfloat16),
            jax.ShapeDtypeStruct((head_size, width), jnp.bfloat16),
            jax.ShapeDtypeStruct((head_size, width), jnp.float32),
            jax.ShapeDtypeStruct((rows, width), jnp.float32),
        ),
        in_specs=[hbm, hbm, hbm, vmem, hbm],
        out_specs=(hbm, hbm, hbm, hbm),
        scratch_shapes=[
            pltpu.VMEM((3, HEADS, tokens, head_size), jnp.bfloat16),
            pltpu.VMEM((3, tokens, HEADS, head_size), jnp.bfloat16),
            pltpu.VMEM((3, HEADS, tokens, head_size), jnp.bfloat16),
            pltpu.VMEM((3, length, head_size), jnp.bfloat16),
            pltpu.VMEM((BLOCKS, tokens, width), jnp.bfloat16),
            pltpu.VMEM((head_size, width), jnp.bfloat16),
            pltpu.VMEM((head_size, width), jnp.float32),
            pltpu.VMEM((BLOCKS, length), jnp.float32),
            pltpu.VMEM((length, head_size), jnp.bfloat16),
            pltpu.VMEM((head_size, length), jnp.float32),
            pltpu.VMEM((head_size, length), jnp.float32),
            pltpu.VMEM((2, length, head_size), jnp.bfloat16),
            pltpu.VMEM((head_size, width), jnp.float32),
            pltpu.VMEM((head_size, width), jnp.bfloat16),
            pltpu.VMEM((head_size, width), jnp.float32),
            pltpu.VMEM((SIDE, 2 * rows, width), jnp.bfloat16),
            pltpu.VMEM((2, rows, width), jnp.bfloat16),
            pltpu.VMEM((2, rows, width), jnp.bfloat16),
            pltpu.VMEM((head_size, width), jnp.bfloat16),
            pltpu.VMEM((rows, width), jnp.float32),
            pltpu.VMEM((head_size, width), jnp.bfloat16),
            pltpu.VMEM((head_size, width), jnp.bfloat16),
            pltpu.VMEM((head_size, width), jnp.float32),
            dma((3,)), dma((BLOCKS,)), dma((BLOCKS,)),
            dma((34,)), dma((34,)),
            dma((BLOCKS,)), dma((BLOCKS,)),
            dma((2,)), dma((3,)),
            dma((BLOCKS,)), dma((BLOCKS,)),
            dma((BLOCKS,)), dma((BLOCKS,)),
            dma((3,)), dma((3,)),
            dma((SIDE - 1,)), dma((SIDE - 1,)),
            dma((2,)), dma((2,)),
            dma((WORKERS - 1,)), dma((WORKERS - 1,)),
            dma((9,)),
        ],
        compiler_params=pltpu.CompilerParams(
            collective_id=0, has_side_effects=True, vmem_limit_bytes=56 << 20
        ),
    )(qkv[:, 0], d_out[0], w_out[0], tile_mask, momentum[0])
    grad_qkv, synced, worker_error, server_error = pl.pallas_call(
        finish,
        out_shape=(
            jax.ShapeDtypeStruct((3, tokens, HEADS, head_size), jnp.bfloat16),
            jax.ShapeDtypeStruct((head_size, width), jnp.bfloat16),
            jax.ShapeDtypeStruct((head_size, width), jnp.float32),
            jax.ShapeDtypeStruct((rows, width), jnp.float32),
        ),
        in_specs=[hbm] * 4,
        out_specs=(hbm,) * 4,
        scratch_shapes=[
            pltpu.VMEM((3, tokens, HEADS, head_size), jnp.bfloat16),
            pltpu.VMEM((head_size, width), jnp.bfloat16),
            pltpu.VMEM((head_size, width), jnp.float32),
            pltpu.VMEM((rows, width), jnp.float32),
            dma((7,)), dma((7,)),
        ],
        compiler_params=pltpu.CompilerParams(vmem_limit_bytes=56 << 20),
    )(grads, synced, worker_error, server_error)
    grad_qkv = grad_qkv[:, None]
    return (grad_qkv, synced[None], worker_error[None, None], server_error[None])


def solution(mesh):
    placed = (
        P(None, "dp", "seq", None, None),
        P(),
        P("dp", "seq", None),
        P("seq", None, None),
        P("seq", None, None),
    )
    return jax.shard_map(
        body,
        mesh=mesh,
        in_specs=placed,
        out_specs=(
            P(None, "dp", "seq", None, None),
            P("seq", None, None),
            P("dp", "seq", None, None),
            P("seq", "dp", None),
        ),
        check_vma=False,
    )
```
